32 devices in a mesh: tm: 8 (over z, y), rows: 4 (over x, core).
Axes of the slice: x: 2, y: 2, z: 4, core: 2. Of those that a mesh axis runs over, the one named last changes fastest.
Arguments:
- phases: bfloat16 [16, 512, 512], P('tm', 'rows'), may hold values from -6 to 6
- focal_data: bfloat16 [16, 2, 256, 256], P('tm', None, 'rows'), may hold values from -6 to 6
- shifts: int32 [16, 2], P('tm'), may hold values from 0 to 2, as said below
- pupil_mask: int32 [512, 512], P('rows'), may hold values 0 or 1
Outputs:
- adjoint_field: float32 [16, 512, 512], P('tm', 'rows')
- wind_grad: float32 [2], replicated
The draws below stay inside these ranges and needn't reach their ends.
Inputs may be any that keep to these rules, and one draw needn't show every extreme that they name: `shifts`: column 0 is a frame's shift along pupil rows, 0 or 1, and sums over all frames to exactly 8; column 1 is its shift along pupil columns, 0 to 2.
All inputs are finite; a program needn't handle non-finite values. No bound on the sum of `pupil_mask` on one device may be relied on, other than what follows from the above.
Results may differ from the reference program's by a relative error of at most 0.0054.
Values may be sent and summed in bfloat16 or wider, within the bound.
No kernel may reach another device: no remote copies, remote signals or barrier semaphores. Data moves between devices by JAX's collectives and lax.ppermute only.
A program may use at most 128 MiB of HBM per device.

```python
import math
import jax
import jax.numpy as jnp
from jax import lax

PUPIL = 512
FOCAL = 256
FRAMES = 16
ROW_SHIFT_SUM = 8


def draw_shifts(key, part):
    rank_key, side_key = jax.random.split(jax.random.fold_in(key, 11))
    ranking = jax.random.permutation(rank_key, FRAMES)
    down_steps = (ranking < ROW_SHIFT_SUM).astype(jnp.int32)
    side_steps = jax.random.randint(side_key, (FRAMES,), 0, 3, dtype=jnp.int32)
    return jnp.stack([down_steps, side_steps], axis=1)


def touch_ends(result, own_key, smallest, high):
    longest = result.shape.index(max(result.shape))
    spots = []
    for shift in (0, 1):
        where = [jax.random.randint(jax.random.fold_in(own_key, axis), (), 0, length) for axis, length in enumerate(result.shape)]
        where[longest] = (where[longest] + shift) % result.shape[longest]
        spots.append(tuple(where))
    return result.at[spots[0]].set(smallest).at[spots[1]].set(high)


def levels(own_key, extent, cuts, least, top_value):
    level, own = 1.0, jax.random.fold_in(own_key, 6)
    for axis_at, blocks in cuts:
        draws = jnp.exp(jax.random.uniform(jax.random.fold_in(own, axis_at), (blocks,), jnp.float32, least / len(cuts), top_value / len(cuts)))
        level = level * jnp.repeat(draws, extent[axis_at] // blocks).reshape([-1 if axis == axis_at else 1 for axis in range(len(extent))])
    return level


def scatter_about(key, shape, scale, most, shards=(), kind=jnp.bfloat16):
    values = jax.random.normal(key, shape, jnp.float32) * scale
    if len(shards) > 0:
        values = levels(key, shape, shards, -0.22, 0.18) * values
    return jnp.clip(values, min=-most, max=most).astype(kind)


def setup_inputs(seed: int = 0) -> dict:
    streams_of = jax.random.split(jax.random.key(seed), 5)
    phases = scatter_about(streams_of[0], (FRAMES, PUPIL, PUPIL), 1.0, 6.0, ((0, 8), (1, 4)))
    focal_data = scatter_about(streams_of[1], (FRAMES, 2, FOCAL, FOCAL), 1.0, 6.0, ((0, 8), (2, 4)))
    shifts = draw_shifts(jax.random.fold_in(streams_of[4], 71), 0)
    pupil_mask = touch_ends((jax.random.randint(streams_of[3], (PUPIL, PUPIL), 0, 10) < 9).astype(jnp.int32), jax.random.fold_in(streams_of[3], 1), 0, 1)
    return {"phases": phases, "focal_data": focal_data, "shifts": shifts, "pupil_mask": pupil_mask}


decay_rate = 0.999

def tables(first_row, row_total):
    focal_pos = jnp.arange(FOCAL, dtype=jnp.int32) - FOCAL // 2
    pupil_pos = first_row + jnp.arange(row_total, dtype=jnp.int32) - PUPIL // 2
    turns = jnp.mod(focal_pos[:, None] * pupil_pos[None, :], 2 * PUPIL)
    angle = turns.astype(jnp.float32) * (math.pi / PUPIL)
    factor = 1.0 / math.sqrt(PUPIL)
    return ((jnp.cos(angle) * factor).astype(jnp.bfloat16), (-jnp.sin(angle) * factor).astype(jnp.bfloat16))

def shift_back(field_in, shift_rows, shift_cols, pad_rows):
    cols_total = field_in.shape[1]
    padded = jnp.pad(field_in, ((0, pad_rows), (0, 0)))
    start_row = jnp.minimum(shift_rows, pad_rows).astype(jnp.int32)
    moved = lax.dynamic_slice(padded, (start_row, jnp.zeros((), jnp.int32)), field_in.shape)
    start_col = jnp.minimum(shift_cols, cols_total).astype(jnp.int32)
    rolled = jnp.roll(moved, -start_col, axis=1)
    keep = jnp.arange(cols_total, dtype=jnp.int32) < cols_total - start_col
    return jnp.where(keep[None, :], rolled, jnp.zeros_like(rolled))

def frame_gradient(phase_now, live, frame_data, cos_t, sin_t):
    masked = jnp.where(live, phase_now, jnp.zeros_like(phase_now))
    y_real = jnp.dot(masked, cos_t.T, preferred_element_type=jnp.float32).astype(jnp.bfloat16)
    y_imag = jnp.dot(masked, sin_t.T, preferred_element_type=jnp.float32).astype(jnp.bfloat16)
    e_real = jnp.dot(cos_t, y_real, preferred_element_type=jnp.float32) - jnp.dot(sin_t, y_imag, preferred_element_type=jnp.float32)
    e_imag = jnp.dot(cos_t, y_imag, preferred_element_type=jnp.float32) + jnp.dot(sin_t, y_real, preferred_element_type=jnp.float32)
    r_real = (frame_data[0].astype(jnp.float32) - e_real).astype(jnp.bfloat16)
    r_imag = (frame_data[1].astype(jnp.float32) - e_imag).astype(jnp.bfloat16)
    w_real = (jnp.dot(cos_t.T, r_real, preferred_element_type=jnp.float32) + jnp.dot(sin_t.T, r_imag, preferred_element_type=jnp.float32)).astype(jnp.bfloat16)
    w_imag = (jnp.dot(cos_t.T, r_imag, preferred_element_type=jnp.float32) - jnp.dot(sin_t.T, r_real, preferred_element_type=jnp.float32)).astype(jnp.bfloat16)
    summed = jnp.dot(w_real, cos_t, preferred_element_type=jnp.float32) + jnp.dot(w_imag, sin_t, preferred_element_type=jnp.float32)
    return jnp.where(live, summed, jnp.zeros_like(summed))

def reference(phases, focal_data, shifts, pupil_mask):
    cos_t, sin_t = tables(0, PUPIL)
    live = pupil_mask == 1

    def backward(carried, inputs):
        lam_next, wind_sum = carried
        phase_now, frame_data, shift_now = inputs
        grad = frame_gradient(phase_now, live, frame_data, cos_t, sin_t)
        prior = decay_rate * shift_back(lam_next, shift_now[0], shift_now[1], PUPIL)
        lam_now = grad + prior
        phase_wide = phase_now.astype(jnp.float32)
        down_diff = jnp.concatenate([phase_wide[1:], jnp.zeros((1, PUPIL), jnp.float32)], axis=0) - phase_wide
        side_diff = jnp.concatenate([phase_wide[:, 1:], jnp.zeros((PUPIL, 1), jnp.float32)], axis=1) - phase_wide
        wind_sum = wind_sum + jnp.stack([jnp.sum(prior * down_diff), jnp.sum(prior * side_diff)])
        return ((lam_now, wind_sum), lam_now)
    start = (jnp.zeros((PUPIL, PUPIL), jnp.float32), jnp.zeros((2,), jnp.float32))
    (last_lam, wind_sum), adjoint_field = lax.scan(backward, start, (phases, focal_data, shifts), reverse=True)
    return (adjoint_field, -wind_sum / (PUPIL * FRAMES))
```

```python
import functools
import math

import jax
import jax.numpy as jnp
import numpy as np
from jax import lax
from jax.experimental import pallas as pl
from jax.experimental.pallas import tpu as pltpu
from jax.sharding import PartitionSpec as P

decay_rate = 0.999
LANES = 128


def tables(pupil, focal):
    focal_pos = np.arange(focal) - focal // 2
    pupil_pos = np.arange(pupil) - pupil // 2
    turns = np.mod(focal_pos[:, None] * pupil_pos[None, :], 2 * pupil)
    angle = turns.astype(np.float32) * np.float32(math.pi / pupil)
    factor = np.float32(1.0 / math.sqrt(pupil))
    cos_t = (np.cos(angle) * factor).astype(jnp.bfloat16)
    sin_t = (-np.sin(angle) * factor).astype(jnp.bfloat16)
    return np.concatenate([cos_t, sin_t], axis=0)


def cum_shifts(sh_ref, stop):
    def add(t, sums):
        return (sums[0] + sh_ref[2 * t], sums[1] + sh_ref[2 * t + 1])

    return lax.fori_loop(0, stop, add, (jnp.int32(0), jnp.int32(0)))


def dot(a, b):
    return jnp.dot(a, b, preferred_element_type=jnp.float32)


def turned(value, down, right):
    value = pltpu.roll(value, lax.rem(down, value.shape[0]), 0)
    return pltpu.roll(value, lax.rem(right, value.shape[1]), 1)


def columns(shape):
    return lax.broadcasted_iota(jnp.int32, shape, 1)


def grad_kernel(
    n_rows, halo, slot, sh_ref, *refs
):
    m_refs, d_refs = refs[:n_rows], refs[n_rows : 2 * n_rows]
    phases_ref, mask_ref, halo_ref, tt_ref, cs_ref = refs[2 * n_rows : 2 * n_rows + 5]
    loc_ref, msg_ref, wind_ref = refs[2 * n_rows + 5 : 2 * n_rows + 8]
    y_ref, d_ref, r_ref, w_ref, lam_ref = refs[2 * n_rows + 8 :]
    frames, block, width = phases_ref.shape
    focal = cs_ref.shape[0] // 2
    part = focal // n_rows
    rows = block + halo
    me = lax.axis_index("rows")
    tm = lax.axis_index("tm")
    for d in range(n_rows):
        at = pl.multiple_of((me ^ d) * block, block)
        y = dot(m_refs[d][...].reshape(frames * block, width), tt_ref[:width])
        y = y.astype(jnp.bfloat16)
        at_q = pl.multiple_of((me ^ d) * part, part)
        for k in range(frames):
            y_ref[k, pl.ds(at, block), :] = y[k * block : (k + 1) * block]
            d_ref[k, :, pl.ds(at_q, part), :] = d_refs[d][k]
    for k in range(frames):
        pq = dot(cs_ref[...], y_ref[k])
        e_real = pq[:focal, :focal] - pq[focal:, focal:]
        e_imag = pq[:focal, focal:] + pq[focal:, :focal]
        real = (d_ref[k, 0].astype(jnp.float32) - e_real).astype(jnp.bfloat16)
        imag = (d_ref[k, 1].astype(jnp.float32) - e_imag).astype(jnp.bfloat16)
        r_ref[:focal, :focal] = real
        r_ref[:focal, focal:] = imag
        r_ref[focal:, :focal] = imag
        r_ref[focal:, focal:] = -real
        rows_t = tt_ref[pl.ds(pl.multiple_of(me * block, block), rows), :]
        w_ref[k] = dot(rows_t, r_ref[...]).astype(jnp.bfloat16)
    live = mask_ref[...] == 1
    live_halo = halo_ref[:halo].astype(jnp.float32) == 1.0
    col = columns((rows, width))
    row = lax.broadcasted_iota(jnp.int32, (rows, width), 0)
    down_sum = jnp.float32(0.0)
    side_sum = jnp.float32(0.0)
    for k in reversed(range(frames)):
        g = dot(w_ref[k], cs_ref[...])
        own = jnp.where(live, g[:block], 0.0)
        over = jnp.where(live_halo, g[block:], 0.0)
        if k == frames - 1:
            loc_ref[k] = own
            lam_ref[:block] = own
            lam_ref[block:] = over
        else:
            t = tm * frames + k
            a = sh_ref[2 * t]
            b = sh_ref[2 * t + 1]
            moved = turned(lam_ref[...], rows - a, width - b)
            inside = (col < width - b) & (row < rows - a)
            prior = jnp.where(inside, decay_rate * moved, 0.0)
            down, side = diffs(phases_ref, halo_ref, halo, k)
            down_sum = down_sum + jnp.sum(prior[:block] * down)
            side_sum = side_sum + jnp.sum(prior[:block] * side)
            own = own + prior[:block]
            loc_ref[k] = own
            lam_ref[:block] = own
            lam_ref[block:] = over + prior[block:]
    wind_ref[0] = down_sum
    wind_ref[1] = side_sum
    a_cum, b_cum = cum_shifts(sh_ref, tm * frames)
    canvas = turned(lam_ref[...], halo - a_cum, width - lax.rem(b_cum, width))
    canvas = jnp.where(row >= halo - a_cum, canvas, 0.0)
    per = rows // slot
    for j in range(msg_ref.shape[0]):
        if j < per * (width // LANES):
            c = j // per
            r = j % per
            msg_ref[j] = canvas[r * slot : (r + 1) * slot, c * LANES : (c + 1) * LANES]
        else:
            msg_ref[j] = jnp.zeros((slot, LANES), jnp.float32)


def diffs(phases_ref, halo_ref, halo, k):
    frames, block, width = phases_ref.shape
    here = phases_ref[k].astype(jnp.float32)
    last = halo_ref[halo + 8 * k : halo + 8 * k + 8].astype(jnp.float32)[:1]
    row = lax.broadcasted_iota(jnp.int32, (block, width), 0)
    below = jnp.where(row == block - 1, last, pltpu.roll(here, block - 1, 0))
    right = jnp.where(columns((block, width)) == width - 1, 0.0, pltpu.roll(here, width - 1, 1))
    return below - here, right - here


def scan_kernel(frames, rows, width, sh_ref, got_ref, out_ref):
    n, slot, _ = got_ref.shape
    me = lax.axis_index("tm")
    flat = me * slot + lax.broadcasted_iota(jnp.int32, (slot, LANES), 0)
    pos = lax.broadcasted_iota(jnp.int32, (slot, LANES), 1)
    for c in range(1, width // LANES):
        pos = pos + jnp.where(flat >= c * rows, LANES, 0)
    weight = decay_rate**frames

    def one(step, carry):
        field, b_cum = carry
        j = n - 1 - step
        out_ref[j] = field
        b_here = jnp.int32(0)
        for k in range(frames):
            b_here = b_here + sh_ref[2 * (j * frames + k) + 1]
        c = pos + lax.rem(b_cum, width)
        c = jnp.where(c >= width, c - width, c)
        field = got_ref[j] + jnp.where(c >= b_here, weight * field, 0.0)
        return field, b_cum - b_here

    _, b_all = cum_shifts(sh_ref, n * frames)
    lax.fori_loop(0, n, one, (jnp.zeros((slot, LANES), jnp.float32), b_all))


def final_kernel(halo, sh_ref, wind_in, got_ref, loc_ref, phases_ref, halo_ref, adj_ref, wind_ref, c_ref):
    frames, block, width = phases_ref.shape
    n, slot, _ = got_ref.shape
    rows = block + halo
    per = rows // slot
    for j in range(min(n, per * (width // LANES))):
        c = j // per
        r = j % per
        c_ref[r * slot : (r + 1) * slot, c * LANES : (c + 1) * LANES] = got_ref[j]
    tm = lax.axis_index("tm")
    a_cum, b_cum = cum_shifts(sh_ref, (tm + 1) * frames)
    down_sum = wind_in[0]
    side_sum = wind_in[1]
    col = columns((block, width))
    b_own = jnp.int32(0)
    for k in reversed(range(frames)):
        t = tm * frames + k
        a_cum = a_cum - sh_ref[2 * t]
        b_cum = b_cum - sh_ref[2 * t + 1]
        b_own = b_own + sh_ref[2 * t + 1]
        moved = turned(c_ref[...], rows - halo + a_cum, b_cum)[:block]
        moved = jnp.where(col < width - b_own, decay_rate ** (frames - k) * moved, 0.0)
        adj_ref[k] = loc_ref[k] + moved
        down, side = diffs(phases_ref, halo_ref, halo, k)
        down_sum = down_sum + jnp.sum(moved * down)
        side_sum = side_sum + jnp.sum(moved * side)
    wind_ref[0] = down_sum
    wind_ref[1] = side_sum


def swap(value, axis, bit):
    count = lax.axis_size(axis)
    return lax.ppermute(value, axis, [(s, s ^ bit) for s in range(count)])


def gather_rows(value):
    count = lax.axis_size("rows")
    held = {0: value}
    bit = count // 2
    while bit:
        held.update({d ^ bit: swap(v, "rows", bit) for d, v in list(held.items())})
        bit //= 2
    return [held[d] for d in range(count)]


def on_device(phases, focal_data, shifts, pupil_mask):
    frames, block, width = phases.shape
    n_rows = lax.axis_size("rows")
    n_tm = lax.axis_size("tm")
    frames_all = frames * n_tm
    focal = focal_data.shape[3]
    halo = min(frames_all // 2, width // (4 * n_rows))
    halo = -(-halo // 16) * 16
    rows = block + halo
    slot = max(1, rows * (width // LANES) // n_tm)
    cs = tables(width, focal)
    tt = np.concatenate([cs.T, np.zeros((halo, 2 * focal), cs.dtype)], axis=0)
    sh_all = lax.all_to_all(
        jnp.broadcast_to(shifts.reshape(1, 2 * frames), (n_tm, 2 * frames)), "tm", 0, 0
    ).reshape(2 * frames_all)
    masked = jnp.where((pupil_mask == 1)[None], phases, jnp.zeros_like(phases))
    m_parts = gather_rows(masked)
    d_parts = gather_rows(focal_data)
    outgoing = jnp.concatenate(
        [pupil_mask[:halo].astype(jnp.bfloat16)] + [phases[k, :8] for k in range(frames)], axis=0
    )
    incoming = lax.ppermute(outgoing, "rows", [(s, s - 1) for s in range(1, n_rows)])
    vmem = pl.BlockSpec(memory_space=pltpu.VMEM)
    smem = pl.BlockSpec(memory_space=pltpu.SMEM)
    field = jax.ShapeDtypeStruct((frames, block, width), jnp.float32)
    message = jax.ShapeDtypeStruct((n_tm, slot, LANES), jnp.float32)
    pair = jax.ShapeDtypeStruct((2,), jnp.float32)
    loc, msg, wind_local = pl.pallas_call(
        functools.partial(grad_kernel, n_rows, halo, slot),
        out_shape=(field, message, pair),
        in_specs=[smem] + [vmem] * (2 * n_rows + 5),
        out_specs=(vmem, vmem, smem),
        scratch_shapes=[
            pltpu.VMEM((frames, width, 2 * focal), jnp.bfloat16),
            pltpu.VMEM((frames, 2, focal, focal), jnp.bfloat16),
            pltpu.VMEM((2 * focal, 2 * focal), jnp.bfloat16),
            pltpu.VMEM((frames, rows, 2 * focal), jnp.bfloat16),
            pltpu.VMEM((rows, width), jnp.float32),
        ],
        name="grad",
    )(sh_all, *m_parts, *d_parts, phases, pupil_mask, incoming, tt, cs)
    got = lax.all_to_all(msg, "tm", 0, 0)
    fields = pl.pallas_call(
        functools.partial(scan_kernel, frames, rows, width),
        out_shape=message,
        in_specs=[smem, vmem],
        out_specs=vmem,
        name="scan",
    )(sh_all, got)
    back = lax.all_to_all(fields, "tm", 0, 0)
    adjoint, wind = pl.pallas_call(
        functools.partial(final_kernel, halo),
        out_shape=(field, pair),
        in_specs=[smem, smem, vmem, vmem, vmem, vmem],
        out_specs=(vmem, smem),
        scratch_shapes=[pltpu.VMEM((rows, width), jnp.float32)],
        name="final",
    )(sh_all, wind_local, back, loc, phases, incoming)
    wind = lax.psum(wind, "rows")
    wind = lax.all_to_all(jnp.broadcast_to(wind[None], (n_tm, 2)), "tm", 0, 0)
    wind_grad = -jnp.sum(wind, axis=0) / (width * frames_all)
    return adjoint, wind_grad


def solution(mesh):
    in_specs = (P("tm", "rows", None), P("tm", None, "rows", None), P("tm", None), P("rows", None))
    out_specs = (P("tm", "rows", None), P())
    return jax.shard_map(
        on_device, mesh=mesh, in_specs=in_specs, out_specs=out_specs, check_vma=False
    )
```

```python
import functools
import math

import jax
import jax.numpy as jnp
import numpy as np
from jax import lax
from jax.experimental import pallas as pl
from jax.experimental.pallas import tpu as pltpu
from jax.sharding import PartitionSpec as P

decay_rate = 0.999
LANES = 128


def tables(pupil, focal):
    focal_pos = np.arange(focal) - focal // 2
    pupil_pos = np.arange(pupil) - pupil // 2
    turns = np.mod(focal_pos[:, None] * pupil_pos[None, :], 2 * pupil)
    angle = turns.astype(np.float32) * np.float32(math.pi / pupil)
    factor = np.float32(1.0 / math.sqrt(pupil))
    cos_t = (np.cos(angle) * factor).astype(jnp.bfloat16)
    sin_t = (-np.sin(angle) * factor).astype(jnp.bfloat16)
    return np.concatenate([cos_t, sin_t], axis=0)


def own_shift(sh_ref, frames, j, k):
    at = 2 * ((j ^ lax.axis_index("tm")) * frames + k)
    return sh_ref[at], sh_ref[at + 1]


def cum_shifts(sh_ref, frames, stop):
    def add(j, sums):
        for k in range(frames):
            a, b = own_shift(sh_ref, frames, j, k)
            sums = (sums[0] + a, sums[1] + b)
        return sums

    return lax.fori_loop(0, stop, add, (jnp.int32(0), jnp.int32(0)))


def dot(a, b):
    return jnp.dot(a, b, preferred_element_type=jnp.float32)


def turned(value, down, right):
    value = pltpu.roll(value, lax.rem(down, value.shape[0]), 0)
    return pltpu.roll(value, lax.rem(right, value.shape[1]), 1)


def columns(shape):
    return lax.broadcasted_iota(jnp.int32, shape, 1)


def grad_kernel(
    n_rows, halo, slot, sh_ref, *refs
):
    m_refs, d_refs = refs[:n_rows], refs[n_rows : 2 * n_rows]
    phases_ref, mask_ref, halo_ref, tt_ref, cs_ref = refs[2 * n_rows : 2 * n_rows + 5]
    loc_ref, msg_ref, wind_ref = refs[2 * n_rows + 5 : 2 * n_rows + 8]
    y_ref, d_ref, r_ref, w_ref, lam_ref = refs[2 * n_rows + 8 :]
    frames, block, width = phases_ref.shape
    focal = cs_ref.shape[0] // 2
    part = focal // n_rows
    rows = block + halo
    me = lax.axis_index("rows")
    tm = lax.axis_index("tm")
    for d in range(n_rows):
        at = pl.multiple_of((me ^ d) * block, block)
        y = dot(m_refs[d][...].reshape(frames * block, width), tt_ref[:width])
        y = y.astype(jnp.bfloat16)
        at_q = pl.multiple_of((me ^ d) * part, part)
        for k in range(frames):
            y_ref[k, pl.ds(at, block), :] = y[k * block : (k + 1) * block]
            d_ref[k, :, pl.ds(at_q, part), :] = d_refs[d][k]
    for k in range(frames):
        pq = dot(cs_ref[...], y_ref[k])
        e_real = pq[:focal, :focal] - pq[focal:, focal:]
        e_imag = pq[:focal, focal:] + pq[focal:, :focal]
        real = (d_ref[k, 0].astype(jnp.float32) - e_real).astype(jnp.bfloat16)
        imag = (d_ref[k, 1].astype(jnp.float32) - e_imag).astype(jnp.bfloat16)
        r_ref[:focal, :focal] = real
        r_ref[:focal, focal:] = imag
        r_ref[focal:, :focal] = imag
        r_ref[focal:, focal:] = -real
        rows_t = tt_ref[pl.ds(pl.multiple_of(me * block, block), rows), :]
        w_ref[k] = dot(rows_t, r_ref[...]).astype(jnp.bfloat16)
    live = mask_ref[...] == 1
    live_halo = halo_ref[:halo].astype(jnp.float32) == 1.0
    col = columns((rows, width))
    row = lax.broadcasted_iota(jnp.int32, (rows, width), 0)
    down_sum = jnp.float32(0.0)
    side_sum = jnp.float32(0.0)
    for k in reversed(range(frames)):
        g = dot(w_ref[k], cs_ref[...])
        own = jnp.where(live, g[:block], 0.0)
        over = jnp.where(live_halo, g[block:], 0.0)
        if k == frames - 1:
            loc_ref[k] = own
            lam_ref[:block] = own
            lam_ref[block:] = over
        else:
            a, b = sh_ref[2 * k], sh_ref[2 * k + 1]
            moved = turned(lam_ref[...], rows - a, width - b)
            inside = (col < width - b) & (row < rows - a)
            prior = jnp.where(inside, decay_rate * moved, 0.0)
            down, side = diffs(phases_ref, halo_ref, halo, k)
            down_sum = down_sum + jnp.sum(prior[:block] * down)
            side_sum = side_sum + jnp.sum(prior[:block] * side)
            own = own + prior[:block]
            loc_ref[k] = own
            lam_ref[:block] = own
            lam_ref[block:] = over + prior[block:]
    wind_ref[0] = down_sum
    wind_ref[1] = side_sum
    a_cum, b_cum = cum_shifts(sh_ref, frames, tm)
    canvas = turned(lam_ref[...], halo - a_cum, width - lax.rem(b_cum, width))
    canvas = jnp.where(row >= halo - a_cum, canvas, 0.0)
    per = rows // slot
    for j in range(msg_ref.shape[0]):
        if j < per * (width // LANES):
            c = j // per
            r = j % per
            msg_ref[j] = canvas[r * slot : (r + 1) * slot, c * LANES : (c + 1) * LANES]
        else:
            msg_ref[j] = jnp.zeros((slot, LANES), jnp.float32)


def diffs(phases_ref, halo_ref, halo, k):
    frames, block, width = phases_ref.shape
    here = phases_ref[k].astype(jnp.float32)
    last = halo_ref[halo + 8 * k : halo + 8 * k + 8].astype(jnp.float32)[:1]
    row = lax.broadcasted_iota(jnp.int32, (block, width), 0)
    below = jnp.where(row == block - 1, last, pltpu.roll(here, block - 1, 0))
    right = jnp.where(columns((block, width)) == width - 1, 0.0, pltpu.roll(here, width - 1, 1))
    return below - here, right - here


def scan_kernel(frames, rows, width, sh_ref, got_ref, out_ref):
    n, slot, _ = got_ref.shape
    me = lax.axis_index("tm")
    flat = me * slot + lax.broadcasted_iota(jnp.int32, (slot, LANES), 0)
    pos = lax.broadcasted_iota(jnp.int32, (slot, LANES), 1)
    for c in range(1, width // LANES):
        pos = pos + jnp.where(flat >= c * rows, LANES, 0)
    weight = decay_rate**frames

    def one(step, carry):
        field, b_cum = carry
        j = n - 1 - step
        out_ref[j] = field
        b_here = jnp.int32(0)
        for k in range(frames):
            b_here = b_here + own_shift(sh_ref, frames, j, k)[1]
        c = pos + lax.rem(b_cum, width)
        c = jnp.where(c >= width, c - width, c)
        field = got_ref[j] + jnp.where(c >= b_here, weight * field, 0.0)
        return field, b_cum - b_here

    _, b_all = cum_shifts(sh_ref, frames, n)
    lax.fori_loop(0, n, one, (jnp.zeros((slot, LANES), jnp.float32), b_all))


def carried(halo, frames, block, width, sh_ref, got_ref, c_ref):
    n, slot, _ = got_ref.shape
    rows = block + halo
    per = rows // slot
    for j in range(min(n, per * (width // LANES))):
        c = j // per
        r = j % per
        c_ref[r * slot : (r + 1) * slot, c * LANES : (c + 1) * LANES] = got_ref[j]
    a_cum, b_cum = cum_shifts(sh_ref, frames, lax.axis_index("tm") + 1)
    col = columns((block, width))
    b_own = jnp.int32(0)
    for k in reversed(range(frames)):
        a, b = sh_ref[2 * k], sh_ref[2 * k + 1]
        a_cum = a_cum - a
        b_cum = b_cum - b
        b_own = b_own + b
        moved = turned(c_ref[...], rows - halo + a_cum, b_cum)[:block]
        yield k, jnp.where(col < width - b_own, decay_rate ** (frames - k) * moved, 0.0)


def wind_kernel(halo, sh_ref, wind_in, got_ref, phases_ref, halo_ref, wind_ref, c_ref):
    frames, block, width = phases_ref.shape
    down_sum = wind_in[0]
    side_sum = wind_in[1]
    for k, moved in carried(halo, frames, block, width, sh_ref, got_ref, c_ref):
        down, side = diffs(phases_ref, halo_ref, halo, k)
        down_sum = down_sum + jnp.sum(moved * down)
        side_sum = side_sum + jnp.sum(moved * side)
    lane = lax.broadcasted_iota(jnp.int32, wind_ref.shape, 2)
    wind_ref[...] = jnp.where(lane == 0, down_sum, jnp.where(lane == 1, side_sum, 0.0))


def final_kernel(halo, sh_ref, got_ref, loc_ref, adj_ref, c_ref):
    frames, block, width = loc_ref.shape
    for k, moved in carried(halo, frames, block, width, sh_ref, got_ref, c_ref):
        adj_ref[k] = loc_ref[k] + moved


def swap(value, axis, bit):
    count = lax.axis_size(axis)
    return lax.ppermute(value, axis, [(s, s ^ bit) for s in range(count)])


def gather_rows(value):
    count = lax.axis_size("rows")
    held = {0: value}
    bit = count // 2
    while bit:
        held.update({d ^ bit: swap(v, "rows", bit) for d, v in list(held.items())})
        bit //= 2
    return [held[d] for d in range(count)]


def on_device(phases, focal_data, shifts, pupil_mask):
    frames, block, width = phases.shape
    n_rows = lax.axis_size("rows")
    n_tm = lax.axis_size("tm")
    frames_all = frames * n_tm
    focal = focal_data.shape[3]
    halo = min(frames_all // 2, width // (4 * n_rows))
    halo = -(-halo // 16) * 16
    rows = block + halo
    slot = max(1, rows * (width // LANES) // n_tm)
    cs = tables(width, focal)
    tt = np.concatenate([cs.T, np.zeros((halo, 2 * focal), cs.dtype)], axis=0)
    sh_all = shifts.reshape(2 * frames)
    bit = 1
    while bit < n_tm:
        sh_all = jnp.concatenate([sh_all, swap(sh_all, "tm", bit)])
        bit *= 2
    masked = jnp.where((pupil_mask == 1)[None], phases, jnp.zeros_like(phases))
    m_parts = gather_rows(masked)
    d_parts = gather_rows(focal_data)
    outgoing = jnp.concatenate(
        [pupil_mask[:halo].astype(jnp.bfloat16)] + [phases[k, :8] for k in range(frames)], axis=0
    )
    incoming = lax.ppermute(outgoing, "rows", [(s, s - 1) for s in range(1, n_rows)])
    vmem = pl.BlockSpec(memory_space=pltpu.VMEM)
    smem = pl.BlockSpec(memory_space=pltpu.SMEM)
    field = jax.ShapeDtypeStruct((frames, block, width), jnp.float32)
    message = jax.ShapeDtypeStruct((n_tm, slot, LANES), jnp.float32)
    pair = jax.ShapeDtypeStruct((2,), jnp.float32)
    loc, msg, wind_local = pl.pallas_call(
        functools.partial(grad_kernel, n_rows, halo, slot),
        out_shape=(field, message, pair),
        in_specs=[smem] + [vmem] * (2 * n_rows + 5),
        out_specs=(vmem, vmem, smem),
        scratch_shapes=[
            pltpu.VMEM((frames, width, 2 * focal), jnp.bfloat16),
            pltpu.VMEM((frames, 2, focal, focal), jnp.bfloat16),
            pltpu.VMEM((2 * focal, 2 * focal), jnp.bfloat16),
            pltpu.VMEM((frames, rows, 2 * focal), jnp.bfloat16),
            pltpu.VMEM((rows, width), jnp.float32),
        ],
        compiler_params=pltpu.CompilerParams(vmem_limit_bytes=28 << 20),
        name="grad",
    )(sh_all, *m_parts, *d_parts, phases, pupil_mask, incoming, tt, cs)
    got = lax.all_to_all(msg, "tm", 0, 0)
    fields = pl.pallas_call(
        functools.partial(scan_kernel, frames, rows, width),
        out_shape=message,
        in_specs=[smem, vmem],
        out_specs=vmem,
        compiler_params=pltpu.CompilerParams(vmem_limit_bytes=6 << 20),
        name="scan",
    )(sh_all, got)
    back = lax.all_to_all(fields, "tm", 0, 0)
    n_all = n_tm * n_rows
    canvas = pltpu.VMEM((rows, width), jnp.float32)
    wind = pl.pallas_call(
        functools.partial(wind_kernel, halo),
        out_shape=jax.ShapeDtypeStruct((n_all, 1, LANES), jnp.float32),
        in_specs=[smem, smem, vmem, vmem, vmem],
        out_specs=vmem,
        scratch_shapes=[canvas],
        compiler_params=pltpu.CompilerParams(vmem_limit_bytes=8 << 20),
        name="wind",
    )(sh_all, wind_local, back, phases, incoming)
    winds = lax.all_to_all(wind, ("tm", "rows"), 0, 0)
    adjoint = pl.pallas_call(
        functools.partial(final_kernel, halo),
        out_shape=field,
        in_specs=[smem, vmem, vmem],
        out_specs=vmem,
        scratch_shapes=[canvas],
        cost_estimate=pl.CostEstimate(
            flops=10 * rows * width, bytes_accessed=12 * frames * block * width, transcendentals=0
        ),
        compiler_params=pltpu.CompilerParams(vmem_limit_bytes=8 << 20),
        name="final",
    )(sh_all, back, loc)
    wind_grad = -jnp.sum(winds[:, 0, :2], axis=0) / (width * frames_all)
    return adjoint, wind_grad


def solution(mesh):
    in_specs = (P("tm", "rows", None), P("tm", None, "rows", None), P("tm", None), P("rows", None))
    out_specs = (P("tm", "rows", None), P())
    return jax.shard_map(
        on_device, mesh=mesh, in_specs=in_specs, out_specs=out_specs, check_vma=False
    )
```

```python
import functools
import math

import jax
import jax.numpy as jnp
import numpy as np
from jax import lax
from jax.experimental import pallas as pl
from jax.experimental.pallas import tpu as pltpu
from jax.sharding import PartitionSpec as P

decay_rate = 0.999
LANES = 128


def tables(pupil, focal):
    focal_pos = np.arange(focal) - focal // 2
    pupil_pos = np.arange(pupil) - pupil // 2
    turns = np.mod(focal_pos[:, None] * pupil_pos[None, :], 2 * pupil)
    angle = turns.astype(np.float32) * np.float32(math.pi / pupil)
    factor = np.float32(1.0 / math.sqrt(pupil))
    cos_t = (np.cos(angle) * factor).astype(jnp.bfloat16)
    sin_t = (-np.sin(angle) * factor).astype(jnp.bfloat16)
    return np.concatenate([cos_t, sin_t], axis=0)


def own_shift(sh_ref, frames, j, k):
    at = 2 * ((j ^ lax.axis_index("tm")) * frames + k)
    return sh_ref[at], sh_ref[at + 1]


def cum_shifts(sh_ref, frames, stop):
    def add(j, sums):
        for k in range(frames):
            a, b = own_shift(sh_ref, frames, j, k)
            sums = (sums[0] + a, sums[1] + b)
        return sums

    return lax.fori_loop(0, stop, add, (jnp.int32(0), jnp.int32(0)))


def dot(a, b):
    return jnp.dot(a, b, preferred_element_type=jnp.float32)


def turned(value, down, right):
    value = pltpu.roll(value, lax.rem(down, value.shape[0]), 0)
    return pltpu.roll(value, lax.rem(right, value.shape[1]), 1)


def columns(shape):
    return lax.broadcasted_iota(jnp.int32, shape, 1)


def y_kernel(halo, phases_ref, mask_ref, half_ref, *refs):
    count = (len(refs) - 2) // 2
    y_ref = refs[count]
    copies = [
        pltpu.make_async_copy(refs[i], refs[count + 1 + i], refs[-1].at[i]) for i in range(count)
    ]
    for copy in copies:
        copy.start()
    frames, block, width = phases_ref.shape
    focal = y_ref.shape[1]
    parts = width // focal
    live = mask_ref[...] == 1
    zero_freq = jnp.full((16, width), zero_freq_value(width), jnp.bfloat16)
    row = lax.broadcasted_iota(jnp.int32, (16, block), 0)
    rows = lax.broadcasted_iota(jnp.int32, (16, focal), 0)
    dc = jnp.zeros((16, block), jnp.float32)
    edge = jnp.zeros((16, focal), jnp.float32)
    for k in range(frames):
        masked = jnp.where(live, phases_ref[k].astype(jnp.float32), 0.0).astype(jnp.bfloat16)
        y_ref[k * block : (k + 1) * block] = dot(masked, half_ref[...]).astype(jnp.bfloat16)
        dc = jnp.where(row == k, dot_t(zero_freq, masked), dc)
        top = phases_ref[k, :8].astype(jnp.float32)[:1]
        for i in range(parts):
            here = jnp.broadcast_to(top[:, i * focal : (i + 1) * focal], edge.shape)
            edge = jnp.where(rows == frames + k * parts + i, here, edge)
    at = frames * block
    y_ref[at : at + 16] = edge.astype(jnp.bfloat16)
    y_ref[at : at + 16, :block] = (edge[:, :block] + dc).astype(jnp.bfloat16)
    at = at + 16
    mask = mask_ref[:halo].astype(jnp.float32).astype(jnp.bfloat16)
    for i in range(parts):
        y_ref[at + i * halo : at + (i + 1) * halo] = mask[:, i * focal : (i + 1) * focal]
    for copy in copies:
        copy.wait()


def zero_freq_value(width):
    return float(np.float32(np.float32(1.0 / math.sqrt(width)).astype(jnp.bfloat16)))


def dot_t(a, b):
    return lax.dot_general(a, b, (((1,), (1,)), ((), ())), preferred_element_type=jnp.float32)


def grad_kernel(n_rows, halo, *refs):
    m_refs, d_refs = refs[:n_rows], refs[n_rows : 2 * n_rows]
    mask_ref, tt_ref, cs_ref, turned_ref, flip_ref = refs[2 * n_rows : 2 * n_rows + 5]
    g_ref, next_ref = refs[2 * n_rows + 5 : 2 * n_rows + 7]
    y_ref, dc_ref, d_ref, r_ref, w_ref, over_ref = refs[2 * n_rows + 7 :]
    frames = w_ref.shape[0]
    block, width = mask_ref.shape
    focal = cs_ref.shape[0] // 2
    parts = width // focal
    half = focal // 2
    part = focal // n_rows
    rows = block + halo
    me = lax.axis_index("rows")
    over_ref[...] = jnp.zeros_like(over_ref)
    next_ref[...] = jnp.zeros_like(next_ref)
    for d in range(1, n_rows):

        @pl.when((me ^ d) == me + 1)
        def _():
            at = frames * block
            edge = m_refs[d][at : at + 16].astype(jnp.float32)
            for k in range(frames):
                for i in range(parts):
                    line = frames + k * parts + i
                    next_ref[k : k + 1, i * focal : (i + 1) * focal] = edge[line : line + 1]
            at = at + 16
            for i in range(parts):
                over_ref[:, i * focal : (i + 1) * focal] = m_refs[d][
                    at + i * halo : at + (i + 1) * halo
                ].astype(jnp.float32)

    for d in range(n_rows):
        at = pl.multiple_of((me ^ d) * block, block)
        at_q = pl.multiple_of((me ^ d) * part, part)
        for k in range(frames):
            y_ref[k, pl.ds(at, block), :] = m_refs[d][k * block : (k + 1) * block]
            d_ref[k, :, pl.ds(at_q, part), :] = d_refs[d][k]
        dc_ref[:, pl.ds(at, block)] = m_refs[d][frames * block : frames * block + 16, :block]
    dc = dot_t(cs_ref[...], dc_ref[...])
    first = columns((focal, half)) == 0
    for k in range(frames):
        pq = dot(cs_ref[...], y_ref[k])
        c_real, c_imag = pq[:focal, :half], pq[:focal, half:]
        s_real, s_imag = pq[focal:, :half], pq[focal:, half:]
        e_real = (c_real - s_imag, jnp.where(first, dc[:focal, k : k + 1], c_real + s_imag))
        e_imag = (c_imag + s_real, jnp.where(first, dc[focal:, k : k + 1], s_real - c_imag))
        for i in range(2):
            at = slice(i * half, (i + 1) * half)
            real, imag = d_ref[k, 0, :, at], d_ref[k, 1, :, at]
            if i:
                real, imag = dot(real, flip_ref[...]), dot(imag, flip_ref[...])
            real = (real.astype(jnp.float32) - e_real[i]).astype(jnp.bfloat16)
            imag = (imag.astype(jnp.float32) - e_imag[i]).astype(jnp.bfloat16)
            r_ref[:focal, i * half : (i + 1) * half] = real
            r_ref[:focal, focal + i * half : focal + (i + 1) * half] = imag
            r_ref[focal:, i * half : (i + 1) * half] = imag
            r_ref[focal:, focal + i * half : focal + (i + 1) * half] = -real
        rows_t = tt_ref[pl.ds(pl.multiple_of(me * block, block), rows), :]
        w_ref[k] = dot(rows_t, r_ref[...]).astype(jnp.bfloat16)
    live = mask_ref[...] == 1
    live_over = over_ref[...] == 1.0
    for k in range(frames):
        g = dot(w_ref[k], turned_ref[...])
        g_ref[k, :block] = jnp.where(live, g[:block], 0.0)
        g_ref[k, block:] = jnp.where(live_over, g[block:], 0.0)


def segment_kernel(slot, sh_ref, g_ref, phases_ref, next_ref, loc_ref, msg_ref, wind_ref):
    frames, rows, width = g_ref.shape
    block = phases_ref.shape[1]
    halo = rows - block
    col = columns((rows, width))
    row = lax.broadcasted_iota(jnp.int32, (rows, width), 0)
    down_sum = jnp.float32(0.0)
    side_sum = jnp.float32(0.0)
    lam = g_ref[frames - 1]
    loc_ref[frames - 1] = lam[:block]
    for k in reversed(range(frames - 1)):
        a, b = sh_ref[2 * k], sh_ref[2 * k + 1]
        inside = (col < width - b) & (row < rows - a)
        prior = jnp.where(inside, decay_rate * turned(lam, rows - a, width - b), 0.0)
        down, side = diffs(phases_ref, next_ref, k)
        down_sum = down_sum + jnp.sum(prior[:block] * down)
        side_sum = side_sum + jnp.sum(prior[:block] * side)
        lam = g_ref[k] + prior
        loc_ref[k] = lam[:block]
    wind_ref[0] = down_sum
    wind_ref[1] = side_sum
    a_cum, b_cum = cum_shifts(sh_ref, frames, lax.axis_index("tm"))
    canvas = turned(lam, halo - a_cum, width - lax.rem(b_cum, width))
    canvas = jnp.where(row >= halo - a_cum, canvas, 0.0)
    per = rows // slot
    for j in range(msg_ref.shape[0]):
        if j < per * (width // LANES):
            c = j // per
            r = j % per
            msg_ref[j] = canvas[r * slot : (r + 1) * slot, c * LANES : (c + 1) * LANES]
        else:
            msg_ref[j] = jnp.zeros((slot, LANES), jnp.float32)


def diffs(phases_ref, next_ref, k):
    frames, block, width = phases_ref.shape
    here = phases_ref[k].astype(jnp.float32)
    last = next_ref[k : k + 1]
    row = lax.broadcasted_iota(jnp.int32, (block, width), 0)
    below = jnp.where(row == block - 1, last, pltpu.roll(here, block - 1, 0))
    right = jnp.where(columns((block, width)) == width - 1, 0.0, pltpu.roll(here, width - 1, 1))
    return below - here, right - here


def scan_kernel(frames, rows, width, sh_ref, got_ref, out_ref):
    n, slot, _ = got_ref.shape
    me = lax.axis_index("tm")
    flat = me * slot + lax.broadcasted_iota(jnp.int32, (slot, LANES), 0)
    pos = lax.broadcasted_iota(jnp.int32, (slot, LANES), 1)
    for c in range(1, width // LANES):
        pos = pos + jnp.where(flat >= c * rows, LANES, 0)
    weight = decay_rate**frames

    def one(step, carry):
        field, b_cum = carry
        j = n - 1 - step
        out_ref[j] = field
        b_here = jnp.int32(0)
        for k in range(frames):
            b_here = b_here + own_shift(sh_ref, frames, j, k)[1]
        c = pos + lax.rem(b_cum, width)
        c = jnp.where(c >= width, c - width, c)
        field = got_ref[j] + jnp.where(c >= b_here, weight * field, 0.0)
        return field, b_cum - b_here

    _, b_all = cum_shifts(sh_ref, frames, n)
    lax.fori_loop(0, n, one, (jnp.zeros((slot, LANES), jnp.float32), b_all))


def carried(halo, frames, block, width, sh_ref, got_ref, c_ref):
    n, slot, _ = got_ref.shape
    rows = block + halo
    per = rows // slot
    for j in range(min(n, per * (width // LANES))):
        c = j // per
        r = j % per
        c_ref[r * slot : (r + 1) * slot, c * LANES : (c + 1) * LANES] = got_ref[j]
    a_cum, b_cum = cum_shifts(sh_ref, frames, lax.axis_index("tm") + 1)
    col = columns((block, width))
    b_own = jnp.int32(0)
    for k in reversed(range(frames)):
        a, b = sh_ref[2 * k], sh_ref[2 * k + 1]
        a_cum = a_cum - a
        b_cum = b_cum - b
        b_own = b_own + b
        moved = turned(c_ref[...], rows - halo + a_cum, b_cum)[:block]
        yield k, jnp.where(col < width - b_own, decay_rate ** (frames - k) * moved, 0.0)


def wind_kernel(halo, sh_ref, wind_in, got_ref, phases_ref, next_ref, wind_ref, c_ref):
    frames, block, width = phases_ref.shape
    down_sum = wind_in[0]
    side_sum = wind_in[1]
    for k, moved in carried(halo, frames, block, width, sh_ref, got_ref, c_ref):
        down, side = diffs(phases_ref, next_ref, k)
        down_sum = down_sum + jnp.sum(moved * down)
        side_sum = side_sum + jnp.sum(moved * side)
    lane = lax.broadcasted_iota(jnp.int32, wind_ref.shape, 2)
    wind_ref[...] = jnp.where(lane == 0, down_sum, jnp.where(lane == 1, side_sum, 0.0))


def final_kernel(halo, sh_ref, got_ref, loc_ref, adj_ref, c_ref):
    frames, block, width = loc_ref.shape
    for k, moved in carried(halo, frames, block, width, sh_ref, got_ref, c_ref):
        adj_ref[k] = loc_ref[k] + moved


def swap(value, axis, bit):
    count = lax.axis_size(axis)
    return lax.ppermute(value, axis, [(s, s ^ bit) for s in range(count)])


def gather_rows(value):
    count = lax.axis_size("rows")
    held = {0: value}
    bit = count // 2
    while bit:
        held.update({d ^ bit: swap(v, "rows", bit) for d, v in list(held.items())})
        bit //= 2
    return [held[d] for d in range(count)]


def on_device(phases, focal_data, shifts, pupil_mask):
    frames, block, width = phases.shape
    n_rows = lax.axis_size("rows")
    n_tm = lax.axis_size("tm")
    frames_all = frames * n_tm
    focal = focal_data.shape[3]
    halo = min(frames_all // 2, width // (4 * n_rows))
    halo = -(-halo // 16) * 16
    rows = block + halo
    slot = max(1, rows * (width // LANES) // n_tm)
    half = focal // 2
    cs = tables(width, focal)
    tt = np.concatenate([cs.T, np.zeros((halo, 2 * focal), cs.dtype)], axis=0)
    order = np.concatenate([np.arange(half), half + (half - np.arange(half)) % half])
    cs_turned = np.concatenate([cs[order], cs[focal + order]], axis=0)
    y_table = np.concatenate([cs[:half], cs[focal : focal + half]], axis=0).T
    flip = np.zeros((half, half), cs.dtype)
    flip[(half - np.arange(half)) % half, np.arange(half)] = 1
    sh_all = shifts.reshape(2 * frames)
    bit = 1
    while bit < n_tm:
        sh_all = jnp.concatenate([sh_all, swap(sh_all, "tm", bit)])
        bit *= 2
    vmem = pl.BlockSpec(memory_space=pltpu.VMEM)
    smem = pl.BlockSpec(memory_space=pltpu.SMEM)
    hbm = pl.BlockSpec(memory_space=pltpu.HBM)
    kept = [tt, cs, cs_turned, flip]
    y, *kept = pl.pallas_call(
        functools.partial(y_kernel, halo),
        out_shape=[
            jax.ShapeDtypeStruct((frames * block + 16 + halo * width // focal, focal), jnp.bfloat16)
        ]
        + [jax.ShapeDtypeStruct(t.shape, jnp.bfloat16) for t in kept],
        in_specs=[vmem] * 3 + [hbm] * len(kept),
        out_specs=[vmem] * (1 + len(kept)),
        scratch_shapes=[pltpu.SemaphoreType.DMA((len(kept),))],
        compiler_params=pltpu.CompilerParams(vmem_limit_bytes=8 << 20),
        name="transform",
    )(*[pltpu.with_memory_space_constraint(t, pltpu.HBM) for t in (phases, pupil_mask, y_table, *kept)])
    d_parts = gather_rows(focal_data)
    m_parts = gather_rows(y)
    field = jax.ShapeDtypeStruct((frames, block, width), jnp.float32)
    message = jax.ShapeDtypeStruct((n_tm, slot, LANES), jnp.float32)
    pair = jax.ShapeDtypeStruct((2,), jnp.float32)
    grads, next_rows = pl.pallas_call(
        functools.partial(grad_kernel, n_rows, halo),
        out_shape=(
            jax.ShapeDtypeStruct((frames, rows, width), jnp.float32),
            jax.ShapeDtypeStruct((-(-frames // 8) * 8, width), jnp.float32),
        ),
        in_specs=[vmem] * (2 * n_rows + 5),
        out_specs=(vmem, vmem),
        scratch_shapes=[
            pltpu.VMEM((frames, width, focal), jnp.bfloat16),
            pltpu.VMEM((16, width), jnp.bfloat16),
            pltpu.VMEM((frames, 2, focal, focal), jnp.bfloat16),
            pltpu.VMEM((2 * focal, 2 * focal), jnp.bfloat16),
            pltpu.VMEM((frames, rows, 2 * focal), jnp.bfloat16),
            pltpu.VMEM((halo, width), jnp.float32),
        ],
        compiler_params=pltpu.CompilerParams(vmem_limit_bytes=24 << 20),
        name="grad",
    )(*m_parts, *d_parts, pupil_mask, *kept)
    loc, msg, wind_local = pl.pallas_call(
        functools.partial(segment_kernel, slot),
        out_shape=(field, message, pair),
        in_specs=[smem, vmem, vmem, vmem],
        out_specs=(vmem, vmem, smem),
        compiler_params=pltpu.CompilerParams(vmem_limit_bytes=12 << 20),
        name="segment",
    )(sh_all, grads, phases, next_rows)
    got = lax.all_to_all(msg, "tm", 0, 0)
    fields = pl.pallas_call(
        functools.partial(scan_kernel, frames, rows, width),
        out_shape=message,
        in_specs=[smem, vmem],
        out_specs=vmem,
        compiler_params=pltpu.CompilerParams(vmem_limit_bytes=6 << 20),
        name="scan",
    )(sh_all, got)
    back = lax.all_to_all(fields, "tm", 0, 0)
    n_all = n_tm * n_rows
    canvas = pltpu.VMEM((rows, width), jnp.float32)
    wind = pl.pallas_call(
        functools.partial(wind_kernel, halo),
        out_shape=jax.ShapeDtypeStruct((n_all, 1, LANES), jnp.float32),
        in_specs=[smem, smem, vmem, vmem, vmem],
        out_specs=vmem,
        scratch_shapes=[canvas],
        compiler_params=pltpu.CompilerParams(vmem_limit_bytes=8 << 20),
        name="wind",
    )(sh_all, wind_local, back, phases, next_rows)
    winds = lax.all_to_all(wind, ("tm", "rows"), 0, 0)
    adjoint = pl.pallas_call(
        functools.partial(final_kernel, halo),
        out_shape=field,
        in_specs=[smem, vmem, vmem],
        out_specs=vmem,
        scratch_shapes=[canvas],
        cost_estimate=pl.CostEstimate(
            flops=10 * rows * width, bytes_accessed=12 * frames * block * width, transcendentals=0
        ),
        compiler_params=pltpu.CompilerParams(vmem_limit_bytes=8 << 20),
        name="final",
    )(sh_all, back, loc)
    wind_grad = -jnp.sum(winds[:, 0, :2], axis=0) / (width * frames_all)
    return adjoint, wind_grad


def solution(mesh):
    in_specs = (P("tm", "rows", None), P("tm", None, "rows", None), P("tm", None), P("rows", None))
    out_specs = (P("tm", "rows", None), P())
    return jax.shard_map(
        on_device, mesh=mesh, in_specs=in_specs, out_specs=out_specs, check_vma=False
    )
```

```python
import functools
import math

import jax
import jax.numpy as jnp
import numpy as np
from jax import lax
from jax.experimental import pallas as pl
from jax.experimental.pallas import tpu as pltpu
from jax.sharding import PartitionSpec as P

decay_rate = 0.999
LANES = 128


def tables(pupil, focal):
    focal_pos = np.arange(focal) - focal // 2
    pupil_pos = np.arange(pupil) - pupil // 2
    turns = np.mod(focal_pos[:, None] * pupil_pos[None, :], 2 * pupil)
    angle = turns.astype(np.float32) * np.float32(math.pi / pupil)
    factor = np.float32(1.0 / math.sqrt(pupil))
    cos_t = (np.cos(angle) * factor).astype(jnp.bfloat16)
    sin_t = (-np.sin(angle) * factor).astype(jnp.bfloat16)
    return np.concatenate([cos_t, sin_t], axis=0)


def own_shift(sh_ref, frames, j, k):
    at = 2 * ((j ^ lax.axis_index("tm")) * frames + k)
    return sh_ref[at], sh_ref[at + 1]


def dot(a, b):
    return jnp.dot(a, b, preferred_element_type=jnp.float32)


def turned(value, down, right):
    value = pltpu.roll(value, lax.rem(down, value.shape[0]), 0)
    return pltpu.roll(value, lax.rem(right, value.shape[1]), 1)


def columns(shape):
    return lax.broadcasted_iota(jnp.int32, shape, 1)


def y_kernel(halo, phases_hbm, mask_hbm, half_hbm, *refs):
    count = (len(refs) - 5) // 2
    y_ref = refs[count]
    phases_ref, mask_ref, half_ref, sem = refs[-4:]
    ins = [(phases_hbm, phases_ref), (mask_hbm, mask_ref), (half_hbm, half_ref)]
    copies = [(refs[i], refs[count + 1 + i]) for i in range(count)]
    copies = [
        pltpu.make_async_copy(src, dst, sem.at[i]) for i, (src, dst) in enumerate(ins + copies)
    ]
    for copy in copies:
        copy.start()
    for copy in copies[:3]:
        copy.wait()
    frames, block, width = phases_ref.shape
    focal = y_ref.shape[1]
    parts = width // focal
    live = mask_ref[...] == 1
    zero_freq = jnp.full((16, width), zero_freq_value(width), jnp.bfloat16)
    row = lax.broadcasted_iota(jnp.int32, (16, block), 0)
    rows = lax.broadcasted_iota(jnp.int32, (16, focal), 0)
    dc = jnp.zeros((16, block), jnp.float32)
    edge = jnp.zeros((16, focal), jnp.float32)
    for k in range(frames):
        masked = jnp.where(live, phases_ref[k].astype(jnp.float32), 0.0).astype(jnp.bfloat16)
        y_ref[k * block : (k + 1) * block] = dot(masked, half_ref[...]).astype(jnp.bfloat16)
        dc = jnp.where(row == k, dot_t(zero_freq, masked), dc)
        top = phases_ref[k, :8].astype(jnp.float32)[:1]
        for i in range(parts):
            here = jnp.broadcast_to(top[:, i * focal : (i + 1) * focal], edge.shape)
            edge = jnp.where(rows == frames + k * parts + i, here, edge)
    at = frames * block
    y_ref[at : at + 16] = edge.astype(jnp.bfloat16)
    y_ref[at : at + 16, :block] = (edge[:, :block] + dc).astype(jnp.bfloat16)
    at = at + 16
    mask = mask_ref[:halo].astype(jnp.float32).astype(jnp.bfloat16)
    for i in range(parts):
        y_ref[at + i * halo : at + (i + 1) * halo] = mask[:, i * focal : (i + 1) * focal]
    for copy in copies[3:]:
        copy.wait()


def zero_freq_value(width):
    return float(np.float32(np.float32(1.0 / math.sqrt(width)).astype(jnp.bfloat16)))


def dot_t(a, b):
    return lax.dot_general(a, b, (((1,), (1,)), ((), ())), preferred_element_type=jnp.float32)


def grad_kernel(n_rows, halo, *refs):
    m_refs, d_refs = refs[:n_rows], refs[n_rows : 2 * n_rows]
    mask_ref, tt_ref, cs_ref, turned_ref, flip_ref = refs[2 * n_rows : 2 * n_rows + 5]
    g_ref, next_ref = refs[2 * n_rows + 5 : 2 * n_rows + 7]
    y_ref, dc_ref, d_ref, r_ref, w_ref, over_ref = refs[2 * n_rows + 7 :]
    frames = w_ref.shape[0]
    block, width = mask_ref.shape
    focal = cs_ref.shape[0] // 2
    parts = width // focal
    half = focal // 2
    part = focal // n_rows
    rows = block + halo
    me = lax.axis_index("rows")
    over_ref[...] = jnp.zeros_like(over_ref)
    next_ref[...] = jnp.zeros_like(next_ref)
    for d in range(1, n_rows):

        @pl.when((me ^ d) == me + 1)
        def _():
            at = frames * block
            edge = m_refs[d][at : at + 16].astype(jnp.float32)
            for k in range(frames):
                for i in range(parts):
                    line = frames + k * parts + i
                    next_ref[k : k + 1, i * focal : (i + 1) * focal] = edge[line : line + 1]
            at = at + 16
            for i in range(parts):
                over_ref[:, i * focal : (i + 1) * focal] = m_refs[d][
                    at + i * halo : at + (i + 1) * halo
                ].astype(jnp.float32)

    for d in range(n_rows):
        at = pl.multiple_of((me ^ d) * block, block)
        at_q = pl.multiple_of((me ^ d) * part, part)
        for k in range(frames):
            y_ref[k, pl.ds(at, block), :] = m_refs[d][k * block : (k + 1) * block]
            d_ref[k, :, pl.ds(at_q, part), :] = d_refs[d][k]
        dc_ref[:, pl.ds(at, block)] = m_refs[d][frames * block : frames * block + 16, :block]
    dc = dot_t(cs_ref[...], dc_ref[...])
    first = columns((focal, half)) == 0
    for k in range(frames):
        pq = dot(cs_ref[...], y_ref[k])
        c_real, c_imag = pq[:focal, :half], pq[:focal, half:]
        s_real, s_imag = pq[focal:, :half], pq[focal:, half:]
        e_real = (c_real - s_imag, jnp.where(first, dc[:focal, k : k + 1], c_real + s_imag))
        e_imag = (c_imag + s_real, jnp.where(first, dc[focal:, k : k + 1], s_real - c_imag))
        for i in range(2):
            at = slice(i * half, (i + 1) * half)
            real, imag = d_ref[k, 0, :, at], d_ref[k, 1, :, at]
            if i:
                real, imag = dot(real, flip_ref[...]), dot(imag, flip_ref[...])
            real = (real.astype(jnp.float32) - e_real[i]).astype(jnp.bfloat16)
            imag = (imag.astype(jnp.float32) - e_imag[i]).astype(jnp.bfloat16)
            r_ref[:focal, i * half : (i + 1) * half] = real
            r_ref[:focal, focal + i * half : focal + (i + 1) * half] = imag
            r_ref[focal:, i * half : (i + 1) * half] = imag
            r_ref[focal:, focal + i * half : focal + (i + 1) * half] = -real
        rows_t = tt_ref[pl.ds(pl.multiple_of(me * block, block), rows), :]
        w_ref[k] = dot(rows_t, r_ref[...]).astype(jnp.bfloat16)
    live = mask_ref[...] == 1
    live_over = over_ref[...] == 1.0
    for k in range(frames):
        g = dot(w_ref[k], turned_ref[...])
        g_ref[k, :block] = jnp.where(live, g[:block], 0.0)
        g_ref[k, block:] = jnp.where(live_over, g[block:], 0.0)


def halves(value, y):
    width = value.shape[1]
    low, high = value[:, : width // 2], value[:, width // 2 :]
    return jnp.where(y == 0, low, high), jnp.where(y == 0, high, low)


def pack(ref, value):
    rows, width = value.shape
    top = jnp.full((8, width), jnp.maximum(jnp.max(jnp.abs(value)), 1e-30))
    power = jnp.ceil(jnp.log2(top))
    ref[:rows] = value * jnp.exp2(-power[:1])
    ref[rows:] = power


def unpack(ref):
    rows = ref.shape[0] - 8
    return ref[:rows] * jnp.exp2(ref[rows : rows + 1])


def dropped(value, pos, width, b_cum, b_here):
    c = pos + lax.rem(b_cum, width)
    c = jnp.where(c >= width, c - width, c)
    return jnp.where(c >= b_here, value, 0.0)


def fill_sums(sh_ref, frames, sums_ref):
    def add(j, sums):
        sums_ref[2 * j] = sums[0]
        sums_ref[2 * j + 1] = sums[1]
        for k in range(frames):
            a, b = own_shift(sh_ref, frames, j, k)
            sums = (sums[0] + a, sums[1] + b)
        return sums

    count = lax.axis_size("tm")
    last = lax.fori_loop(0, count, add, (jnp.int32(0), jnp.int32(0)))
    sums_ref[2 * count] = last[0]
    sums_ref[2 * count + 1] = last[1]


def segment_kernel(
    sh_ref, g_ref, phases_ref, next_ref, loc_ref, keep_ref, send_ref, wind_ref, sums_ref
):
    frames, rows, width = g_ref.shape
    block = phases_ref.shape[1]
    halo = rows - block
    tm = lax.axis_index("tm")
    col = columns((rows, width))
    row = lax.broadcasted_iota(jnp.int32, (rows, width), 0)
    down_sum = jnp.float32(0.0)
    side_sum = jnp.float32(0.0)
    lam = g_ref[frames - 1]
    loc_ref[frames - 1] = lam[:block]
    for k in reversed(range(frames - 1)):
        a, b = sh_ref[2 * k], sh_ref[2 * k + 1]
        inside = (col < width - b) & (row < rows - a)
        prior = jnp.where(inside, decay_rate * turned(lam, rows - a, width - b), 0.0)
        down, side = diffs(phases_ref, next_ref, k)
        down_sum = down_sum + jnp.sum(prior[:block] * down)
        side_sum = side_sum + jnp.sum(prior[:block] * side)
        lam = g_ref[k] + prior
        loc_ref[k] = lam[:block]
    wind_ref[0] = down_sum
    wind_ref[1] = side_sum
    fill_sums(sh_ref, frames, sums_ref)
    a_cum, b_cum = sums_ref[2 * tm], sums_ref[2 * tm + 1]
    canvas = turned(lam, halo - a_cum, width - lax.rem(b_cum, width))
    canvas = jnp.where(row >= halo - a_cum, canvas, 0.0)
    keep, send = halves(canvas, tm % 2)
    keep_ref[...] = keep
    pack(send_ref, send)


def z_kernel(halo, sh_ref, sums_ref, phases_ref, next_ref, after_ref, keep_ref, send_ref):
    frames, block, width = phases_ref.shape
    tm = lax.axis_index("tm")
    a_cum, b_cum = sums_ref[2 * tm + 2], sums_ref[2 * tm + 3]
    b_own = jnp.int32(0)
    col = columns((block, width))
    pad = jnp.zeros((halo, width), jnp.float32)
    sums = [jnp.zeros((block + halo, width), jnp.float32) for _ in range(2)]
    for k in reversed(range(frames)):
        a, b = sh_ref[2 * k], sh_ref[2 * k + 1]
        a_cum = a_cum - a
        b_cum = b_cum - b
        b_own = b_own + b
        for i, diff in enumerate(diffs(phases_ref, next_ref, k)):
            diff = jnp.where(col < width - b_own, decay_rate ** (frames - k) * diff, 0.0)
            diff = jnp.concatenate([diff, pad], axis=0)
            sums[i] = sums[i] + turned(diff, halo - a_cum, width - lax.rem(b_cum, width))
    for i in range(2):
        keep, send = halves(sums[i], tm % 2)
        keep_ref[i] = keep
        pack(send_ref.at[i], send)


def combine_kernel(frames, width, sums_ref, keep_ref, got_ref, late_ref, both_ref, send_ref):
    rows, part = keep_ref.shape
    tm = lax.axis_index("tm")
    pair, y = tm // 2, tm % 2
    keep, got = keep_ref[...], unpack(got_ref)
    early = jnp.where(y == 0, keep, got)
    late = jnp.where(y == 0, got, keep)
    late_ref[...] = late
    b_from, b_cum = sums_ref[4 * pair + 1], sums_ref[4 * pair + 3]
    pos = columns((rows, part)) + y * part
    both = early + dropped(decay_rate**frames * late, pos, width, b_cum, b_cum - b_from)
    both_ref[...] = both
    pack(send_ref, both)


def later_pairs(frames, width, reach, sums_ref, got_ref):
    rows = got_ref.shape[0] - 8
    part = got_ref.shape[1]
    tm = lax.axis_index("tm")
    pair, y = tm // 2, tm % 2
    pos = columns((rows, part)) + y * part
    pairs = lax.axis_size("tm") // 2
    got = jnp.where(pair + reach < pairs, unpack(got_ref), 0.0)
    b_cum = sums_ref[4 * jnp.minimum(pair + reach, pairs) + 1]
    b_from, b_next = sums_ref[4 * pair + 1], sums_ref[4 * pair + 5]
    weight = decay_rate ** (2 * frames * reach)
    weight_next = decay_rate ** (2 * frames * (reach - 1))
    incl = dropped(weight * got, pos, width, b_cum, b_cum - b_from)
    return incl, dropped(weight_next * got, pos, width, b_cum, b_cum - b_next)


def step_kernel(frames, width, reach, sums_ref, both_ref, got_ref, *refs):
    incl, excl = later_pairs(frames, width, reach, sums_ref, got_ref)
    incl_ref, excl_ref, send_ref = refs[-3:]
    both = both_ref[...] + incl
    incl_ref[...] = both
    excl_ref[...] = excl + refs[0][...] if len(refs) == 4 else excl
    pack(send_ref, both)


def carry_kernel(frames, width, reach, sums_ref, late_ref, got_ref, *refs):
    keep_ref, send_ref, raw_ref = refs[-3:]
    rows, part = late_ref.shape
    tm = lax.axis_index("tm")
    pair, y = tm // 2, tm % 2
    _, late = later_pairs(frames, width, reach, sums_ref, got_ref)
    if len(refs) == 4:
        late = late + refs[0][...]
    b_from, b_cum = sums_ref[4 * pair + 3], sums_ref[4 * pair + 5]
    pos = columns((rows, part)) + y * part
    moved = dropped(decay_rate**frames * late, pos, width, b_cum, b_cum - b_from)
    early = late_ref[...] + moved
    keep_ref[...] = jnp.where(y == 0, early, late)
    send = jnp.where(y == 0, late, early)
    raw_ref[...] = send
    pack(send_ref, send)


def wind_kernel(wind_in, keep_ref, send_ref, z_ref, zgot_ref, wind_ref):
    sums = [
        wind_in[i]
        + jnp.sum(keep_ref[...] * z_ref[i] + send_ref[...] * unpack(zgot_ref.at[i]))
        for i in range(2)
    ]
    lane = lax.broadcasted_iota(jnp.int32, wind_ref.shape, 2)
    wind_ref[...] = jnp.where(lane == 0, sums[0], jnp.where(lane == 1, sums[1], 0.0))


def final_kernel(sh_ref, sums_ref, keep_ref, got_ref, loc_ref, adj_ref):
    frames, block, width = loc_ref.shape
    rows = keep_ref.shape[0]
    halo = rows - block
    tm = lax.axis_index("tm")
    keep, got = keep_ref[...], unpack(got_ref)
    low = jnp.where(tm % 2 == 0, keep, got)
    high = jnp.where(tm % 2 == 0, got, keep)
    canvas = jnp.concatenate([low, high], axis=1)
    a_cum, b_cum = sums_ref[2 * tm + 2], sums_ref[2 * tm + 3]
    col = columns((block, width))
    b_own = jnp.int32(0)
    for k in reversed(range(frames)):
        a, b = sh_ref[2 * k], sh_ref[2 * k + 1]
        a_cum = a_cum - a
        b_cum = b_cum - b
        b_own = b_own + b
        moved = turned(canvas, rows - halo + a_cum, b_cum)[:block]
        moved = jnp.where(col < width - b_own, decay_rate ** (frames - k) * moved, 0.0)
        adj_ref[k] = loc_ref[k] + moved


def diffs(phases_ref, next_ref, k):
    _, block, width = phases_ref.shape
    here = phases_ref[k].astype(jnp.float32)
    last = next_ref[k : k + 1]
    row = lax.broadcasted_iota(jnp.int32, (block, width), 0)
    below = jnp.where(row == block - 1, last, pltpu.roll(here, block - 1, 0))
    right = jnp.where(columns((block, width)) == width - 1, 0.0, pltpu.roll(here, width - 1, 1))
    return below - here, right - here


def swap(value, axis, bit):
    count = lax.axis_size(axis)
    return lax.ppermute(value, axis, [(s, s ^ bit) for s in range(count)])


def gather_rows(value):
    count = lax.axis_size("rows")
    held = {0: value}
    bit = count // 2
    while bit:
        held.update({d ^ bit: swap(v, "rows", bit) for d, v in list(held.items())})
        bit //= 2
    return [held[d] for d in range(count)]


def from_later(value, pairs_away):
    count = lax.axis_size("tm")
    route = [(s, s - 2 * pairs_away) for s in range(2 * pairs_away, count)]
    return lax.ppermute(value.astype(jnp.float16), "tm", route).astype(jnp.float32)


def swap_half(value):
    return swap(value.astype(jnp.float16), "tm", 1).astype(jnp.float32)


def kernel_call(body, vmem_mib, out_shape, in_specs, out_specs, cost=0):
    estimate = pl.CostEstimate(flops=0, bytes_accessed=cost, transcendentals=0) if cost else None
    return pl.pallas_call(
        body,
        out_shape=out_shape,
        in_specs=in_specs,
        out_specs=out_specs,
        cost_estimate=estimate,
        compiler_params=pltpu.CompilerParams(vmem_limit_bytes=vmem_mib << 20),
    )


def on_device(phases, focal_data, shifts, pupil_mask):
    frames, block, width = phases.shape
    n_rows = lax.axis_size("rows")
    n_tm = lax.axis_size("tm")
    frames_all = frames * n_tm
    focal = focal_data.shape[3]
    halo = min(frames_all // 2, width // (4 * n_rows))
    halo = -(-halo // 16) * 16
    rows = block + halo
    part = width // 2
    pairs = n_tm // 2
    half = focal // 2
    cs = tables(width, focal)
    tt = np.concatenate([cs.T, np.zeros((halo, 2 * focal), cs.dtype)], axis=0)
    order = np.concatenate([np.arange(half), half + (half - np.arange(half)) % half])
    cs_turned = np.concatenate([cs[order], cs[focal + order]], axis=0)
    y_table = np.concatenate([cs[:half], cs[focal : focal + half]], axis=0).T
    flip = np.zeros((half, half), cs.dtype)
    flip[(half - np.arange(half)) % half, np.arange(half)] = 1
    sh_all = shifts.reshape(2 * frames)
    bit = 1
    while bit < n_tm:
        sh_all = jnp.concatenate([sh_all, swap(sh_all, "tm", bit)])
        bit *= 2
    vmem = pl.BlockSpec(memory_space=pltpu.VMEM)
    smem = pl.BlockSpec(memory_space=pltpu.SMEM)
    hbm = pl.BlockSpec(memory_space=pltpu.HBM)
    kept = [tt, cs, cs_turned, flip]
    y, *kept = pl.pallas_call(
        functools.partial(y_kernel, halo),
        out_shape=[
            jax.ShapeDtypeStruct((frames * block + 16 + halo * width // focal, focal), jnp.bfloat16)
        ]
        + [jax.ShapeDtypeStruct(t.shape, jnp.bfloat16) for t in kept],
        in_specs=[hbm] * (3 + len(kept)),
        out_specs=[vmem] * (1 + len(kept)),
        scratch_shapes=[
            pltpu.VMEM(phases.shape, phases.dtype),
            pltpu.VMEM(pupil_mask.shape, pupil_mask.dtype),
            pltpu.VMEM(y_table.shape, y_table.dtype),
            pltpu.SemaphoreType.DMA((3 + len(kept),)),
        ],
        compiler_params=pltpu.CompilerParams(vmem_limit_bytes=8 << 20),
        name="transform",
    )(*[pltpu.with_memory_space_constraint(t, pltpu.HBM) for t in (phases, pupil_mask, y_table, *kept)])
    d_parts = gather_rows(focal_data)
    m_parts = gather_rows(y)
    field = jax.ShapeDtypeStruct((frames, block, width), jnp.float32)
    pair = jax.ShapeDtypeStruct((2,), jnp.float32)
    grads, next_rows = pl.pallas_call(
        functools.partial(grad_kernel, n_rows, halo),
        out_shape=(
            jax.ShapeDtypeStruct((frames, rows, width), jnp.float32),
            jax.ShapeDtypeStruct((-(-frames // 8) * 8, width), jnp.float32),
        ),
        in_specs=[vmem] * (2 * n_rows + 5),
        out_specs=(vmem, vmem),
        scratch_shapes=[
            pltpu.VMEM((frames, width, focal), jnp.bfloat16),
            pltpu.VMEM((16, width), jnp.bfloat16),
            pltpu.VMEM((frames, 2, focal, focal), jnp.bfloat16),
            pltpu.VMEM((2 * focal, 2 * focal), jnp.bfloat16),
            pltpu.VMEM((frames, rows, 2 * focal), jnp.bfloat16),
            pltpu.VMEM((halo, width), jnp.float32),
        ],
        compiler_params=pltpu.CompilerParams(vmem_limit_bytes=24 << 20),
        name="grad",
    )(*m_parts, *d_parts, pupil_mask, *kept)
    half_field = jax.ShapeDtypeStruct((rows, part), jnp.float32)
    message = jax.ShapeDtypeStruct((rows + 8, part), jnp.float32)
    loc, keep, send, wind_local, sums_all = kernel_call(
        segment_kernel, 12,
        (field, half_field, message, pair, jax.ShapeDtypeStruct((2 * n_tm + 2,), jnp.int32)),
        [smem, vmem, vmem, vmem], (vmem, vmem, vmem, smem, smem),
    )(sh_all, grads, phases, next_rows)
    late, both, send = kernel_call(
        functools.partial(combine_kernel, frames, width), 6,
        (half_field, half_field, message), [smem, vmem, vmem], (vmem, vmem, vmem),
    )(sums_all, keep, swap_half(send))
    z_keep, z_send = kernel_call(
        functools.partial(z_kernel, halo), 12,
        (
            jax.ShapeDtypeStruct((2, rows, part), jnp.float32),
            jax.ShapeDtypeStruct((2, rows + 8, part), jnp.float32),
        ),
        [smem, smem, vmem, vmem, pl.BlockSpec(memory_space=pl.ANY)], (vmem, vmem),
    )(sh_all, sums_all, phases, next_rows, late)
    z_got = swap_half(z_send)
    sums = []
    reach = 1
    while 2 * reach < pairs:
        both, excl, send = kernel_call(
            functools.partial(step_kernel, frames, width, reach), 6,
            (half_field, half_field, message),
            [smem] + [vmem] * (2 + len(sums)), (vmem, vmem, vmem),
        )(sums_all, both, from_later(send, reach), *sums)
        sums = [excl]
        reach *= 2
    keep, send, raw = kernel_call(
        functools.partial(carry_kernel, frames, width, reach), 6,
        (half_field, message, half_field),
        [smem] + [vmem] * (2 + len(sums)), (vmem, vmem, vmem),
    )(sums_all, late, from_later(send, reach), *sums)
    got = swap_half(send)
    n_all = n_tm * n_rows
    wind = kernel_call(
        wind_kernel, 6,
        jax.ShapeDtypeStruct((n_all, 1, LANES), jnp.float32),
        [smem] + [vmem] * 4, vmem,
    )(wind_local, keep, raw, z_keep, z_got)
    winds = lax.all_to_all(wind, ("tm", "rows"), 0, 0)
    adjoint = kernel_call(
        final_kernel, 8, field, [smem, smem, vmem, vmem, vmem], vmem,
        cost=12 * frames * block * width,
    )(sh_all, sums_all, keep, got, loc)
    wind_grad = -jnp.sum(winds[:, 0, :2], axis=0) / (width * frames_all)
    return adjoint, wind_grad


def solution(mesh):
    in_specs = (P("tm", "rows", None), P("tm", None, "rows", None), P("tm", None), P("rows", None))
    out_specs = (P("tm", "rows", None), P())

    return jax.shard_map(
        on_device, mesh=mesh, in_specs=in_specs, out_specs=out_specs, check_vma=False
    )
```

```python
import functools
import math

import jax
import jax.numpy as jnp
import numpy as np
from jax import lax
from jax.experimental import pallas as pl
from jax.experimental.pallas import tpu as pltpu
from jax.sharding import PartitionSpec as P

decay_rate = 0.999
LANES = 128


def tables(pupil, focal):
    focal_pos = np.arange(focal) - focal // 2
    pupil_pos = np.arange(pupil) - pupil // 2
    turns = np.mod(focal_pos[:, None] * pupil_pos[None, :], 2 * pupil)
    angle = turns.astype(np.float32) * np.float32(math.pi / pupil)
    factor = np.float32(1.0 / math.sqrt(pupil))
    cos_t = (np.cos(angle) * factor).astype(jnp.bfloat16)
    sin_t = (-np.sin(angle) * factor).astype(jnp.bfloat16)
    return np.concatenate([cos_t, sin_t], axis=0)


def own_shift(sh_ref, frames, j, k):
    at = 2 * ((j ^ lax.axis_index("tm")) * frames + k)
    return sh_ref[at], sh_ref[at + 1]


def dot(a, b):
    return jnp.dot(a, b, preferred_element_type=jnp.float32)


def turned(value, down, right):
    value = pltpu.roll(value, lax.rem(down, value.shape[0]), 0)
    return pltpu.roll(value, lax.rem(right, value.shape[1]), 1)


def columns(shape):
    return lax.broadcasted_iota(jnp.int32, shape, 1)


def y_kernel(halo, phases_hbm, mask_hbm, half_hbm, *refs):
    count = (len(refs) - 5) // 2
    y_ref = refs[count]
    phases_ref, mask_ref, half_ref, sem = refs[-4:]
    ins = [(phases_hbm, phases_ref), (mask_hbm, mask_ref), (half_hbm, half_ref)]
    copies = [(refs[i], refs[count + 1 + i]) for i in range(count)]
    copies = [
        pltpu.make_async_copy(src, dst, sem.at[i]) for i, (src, dst) in enumerate(ins + copies)
    ]
    for copy in copies:
        copy.start()
    for copy in copies[:3]:
        copy.wait()
    frames, block, width = phases_ref.shape
    focal = y_ref.shape[1]
    parts = width // focal
    live = mask_ref[...] == 1
    zero_freq = jnp.full((16, width), zero_freq_value(width), jnp.bfloat16)
    row = lax.broadcasted_iota(jnp.int32, (16, block), 0)
    rows = lax.broadcasted_iota(jnp.int32, (16, focal), 0)
    dc = jnp.zeros((16, block), jnp.float32)
    edge = jnp.zeros((16, focal), jnp.float32)
    for k in range(frames):
        masked = jnp.where(live, phases_ref[k].astype(jnp.float32), 0.0).astype(jnp.bfloat16)
        y_ref[k * block : (k + 1) * block] = dot(masked, half_ref[...]).astype(jnp.bfloat16)
        dc = jnp.where(row == k, dot_t(zero_freq, masked), dc)
        top = phases_ref[k, :8].astype(jnp.float32)[:1]
        for i in range(parts):
            here = jnp.broadcast_to(top[:, i * focal : (i + 1) * focal], edge.shape)
            edge = jnp.where(rows == frames + k * parts + i, here, edge)
    at = frames * block
    y_ref[at : at + 16] = edge.astype(jnp.bfloat16)
    y_ref[at : at + 16, :block] = (edge[:, :block] + dc).astype(jnp.bfloat16)
    at = at + 16
    mask = mask_ref[:halo].astype(jnp.float32).astype(jnp.bfloat16)
    for i in range(parts):
        y_ref[at + i * halo : at + (i + 1) * halo] = mask[:, i * focal : (i + 1) * focal]
    for copy in copies[3:]:
        copy.wait()


def zero_freq_value(width):
    return float(np.float32(np.float32(1.0 / math.sqrt(width)).astype(jnp.bfloat16)))


def dot_t(a, b):
    return lax.dot_general(a, b, (((1,), (1,)), ((), ())), preferred_element_type=jnp.float32)


def grad_kernel(n_rows, halo, *refs):
    m_refs, d_refs = refs[:n_rows], refs[n_rows : 2 * n_rows]
    mask_ref, tt_ref, cs_ref, turned_ref, flip_ref = refs[2 * n_rows : 2 * n_rows + 5]
    g_ref, next_ref = refs[2 * n_rows + 5 : 2 * n_rows + 7]
    y_ref, dc_ref, d_ref, r_ref, w_ref, over_ref = refs[2 * n_rows + 7 :]
    frames = w_ref.shape[0]
    block, width = mask_ref.shape
    focal = cs_ref.shape[0] // 2
    parts = width // focal
    half = focal // 2
    part = focal // n_rows
    rows = block + halo
    me = lax.axis_index("rows")
    over_ref[...] = jnp.zeros_like(over_ref)
    next_ref[...] = jnp.zeros_like(next_ref)
    for d in range(1, n_rows):

        @pl.when((me ^ d) == me + 1)
        def _():
            at = frames * block
            edge = m_refs[d][at : at + 16].astype(jnp.float32)
            for k in range(frames):
                for i in range(parts):
                    line = frames + k * parts + i
                    next_ref[k : k + 1, i * focal : (i + 1) * focal] = edge[line : line + 1]
            at = at + 16
            for i in range(parts):
                over_ref[:, i * focal : (i + 1) * focal] = m_refs[d][
                    at + i * halo : at + (i + 1) * halo
                ].astype(jnp.float32)

    for d in range(n_rows):
        at = pl.multiple_of((me ^ d) * block, block)
        at_q = pl.multiple_of((me ^ d) * part, part)
        for k in range(frames):
            y_ref[k, pl.ds(at, block), :] = m_refs[d][k * block : (k + 1) * block]
            d_ref[k, :, pl.ds(at_q, part), :] = d_refs[d][k]
        dc_ref[:, pl.ds(at, block)] = m_refs[d][frames * block : frames * block + 16, :block]
    dc = dot_t(cs_ref[...], dc_ref[...])
    first = columns((focal, half)) == 0
    for k in range(frames):
        pq = dot(cs_ref[...], y_ref[k])
        c_real, c_imag = pq[:focal, :half], pq[:focal, half:]
        s_real, s_imag = pq[focal:, :half], pq[focal:, half:]
        e_real = (c_real - s_imag, jnp.where(first, dc[:focal, k : k + 1], c_real + s_imag))
        e_imag = (c_imag + s_real, jnp.where(first, dc[focal:, k : k + 1], s_real - c_imag))
        for i in range(2):
            at = slice(i * half, (i + 1) * half)
            real, imag = d_ref[k, 0, :, at], d_ref[k, 1, :, at]
            if i:
                real, imag = dot(real, flip_ref[...]), dot(imag, flip_ref[...])
            real = (real.astype(jnp.float32) - e_real[i]).astype(jnp.bfloat16)
            imag = (imag.astype(jnp.float32) - e_imag[i]).astype(jnp.bfloat16)
            r_ref[:focal, i * half : (i + 1) * half] = real
            r_ref[:focal, focal + i * half : focal + (i + 1) * half] = imag
            r_ref[focal:, i * half : (i + 1) * half] = imag
            r_ref[focal:, focal + i * half : focal + (i + 1) * half] = -real
        rows_t = tt_ref[pl.ds(pl.multiple_of(me * block, block), rows), :]
        w_ref[k] = dot(rows_t, r_ref[...]).astype(jnp.bfloat16)
    live = mask_ref[...] == 1
    live_over = over_ref[...] == 1.0
    for k in range(frames):
        g = dot(w_ref[k], turned_ref[...])
        g_ref[k, :block] = jnp.where(live, g[:block], 0.0)
        g_ref[k, block:] = jnp.where(live_over, g[block:], 0.0)


def halves(value, y):
    width = value.shape[1]
    low, high = value[:, : width // 2], value[:, width // 2 :]
    return jnp.where(y == 0, low, high), jnp.where(y == 0, high, low)


def exponent(value, width):
    top = jnp.full((8, width), jnp.maximum(jnp.max(jnp.abs(value)), 1e-30))
    return jnp.ceil(jnp.log2(top))


def pack(ref, value, power):
    rows = value.shape[0]
    ref[:rows] = value * jnp.exp2(-power[:1])
    ref[rows:] = power


def unpack(ref):
    rows = ref.shape[0] - 8
    return ref[:rows] * jnp.exp2(ref[rows : rows + 1])


def dropped(value, pos, width, b_cum, b_here):
    c = pos + lax.rem(b_cum, width)
    c = jnp.where(c >= width, c - width, c)
    return jnp.where(c >= b_here, value, 0.0)


def fill_sums(sh_ref, frames, sums_ref):
    def add(j, sums):
        sums_ref[2 * j] = sums[0]
        sums_ref[2 * j + 1] = sums[1]
        for k in range(frames):
            a, b = own_shift(sh_ref, frames, j, k)
            sums = (sums[0] + a, sums[1] + b)
        return sums

    count = lax.axis_size("tm")
    last = lax.fori_loop(0, count, add, (jnp.int32(0), jnp.int32(0)))
    sums_ref[2 * count] = last[0]
    sums_ref[2 * count + 1] = last[1]


def segment_kernel(sh_ref, g_ref, loc_ref, keep_ref, send_ref, sums_ref):
    frames, rows, width = g_ref.shape
    block = loc_ref.shape[1]
    halo = rows - block
    tm = lax.axis_index("tm")
    col = columns((rows, width))
    row = lax.broadcasted_iota(jnp.int32, (rows, width), 0)
    lam = g_ref[frames - 1]
    loc_ref[frames - 1] = lam[:block]
    for k in reversed(range(frames - 1)):
        a, b = sh_ref[2 * k], sh_ref[2 * k + 1]
        inside = (col < width - b) & (row < rows - a)
        prior = jnp.where(inside, decay_rate * turned(lam, rows - a, width - b), 0.0)
        lam = g_ref[k] + prior
        loc_ref[k] = lam[:block]
    fill_sums(sh_ref, frames, sums_ref)
    a_cum, b_cum = sums_ref[2 * tm], sums_ref[2 * tm + 1]
    power = exponent(lam, width // 2)
    canvas = turned(lam, halo - a_cum, width - lax.rem(b_cum, width))
    canvas = jnp.where(row >= halo - a_cum, canvas, 0.0)
    keep, send = halves(canvas, tm % 2)
    keep_ref[...] = keep
    pack(send_ref, send, power)


def z_kernel(
    halo, sh_ref, sums_ref, phases_ref, next_ref, g_ref, loc_ref, after_ref,
    keep_ref, send_ref, wind_ref,
):
    frames, block, width = phases_ref.shape
    tm = lax.axis_index("tm")
    a_cum, b_cum = sums_ref[2 * tm + 2], sums_ref[2 * tm + 3]
    b_own = jnp.int32(0)
    col = columns((block, width))
    pad = jnp.zeros((halo, width), jnp.float32)
    sums = [jnp.zeros((block + halo, width), jnp.float32) for _ in range(2)]
    winds = [jnp.float32(0.0), jnp.float32(0.0)]
    for k in reversed(range(frames)):
        a, b = sh_ref[2 * k], sh_ref[2 * k + 1]
        a_cum = a_cum - a
        b_cum = b_cum - b
        b_own = b_own + b
        for i, diff in enumerate(diffs(phases_ref, next_ref, k)):
            if k < frames - 1:
                winds[i] = winds[i] + jnp.sum((loc_ref[k] - g_ref[k, :block]) * diff)
            diff = jnp.where(col < width - b_own, decay_rate ** (frames - k) * diff, 0.0)
            diff = jnp.concatenate([diff, pad], axis=0)
            sums[i] = sums[i] + turned(diff, halo - a_cum, width - lax.rem(b_cum, width))
    for i in range(2):
        keep, send = halves(sums[i], tm % 2)
        keep_ref[i] = keep
        pack(send_ref.at[i], send, exponent(send, width // 2))
        wind_ref[i] = winds[i]


def combine_kernel(
    frames, width, sums_ref, keep_ref, sent_ref, got_ref, late_ref, both_ref, send_ref
):
    rows, part = keep_ref.shape
    tm = lax.axis_index("tm")
    pair, y = tm // 2, tm % 2
    keep, got = keep_ref[...], unpack(got_ref)
    early = jnp.where(y == 0, keep, got)
    late = jnp.where(y == 0, got, keep)
    late_ref[...] = late
    b_from, b_cum = sums_ref[4 * pair + 1], sums_ref[4 * pair + 3]
    pos = columns((rows, part)) + y * part
    both = early + dropped(decay_rate**frames * late, pos, width, b_cum, b_cum - b_from)
    both_ref[...] = both
    pack(send_ref, both, jnp.maximum(sent_ref[rows:], got_ref[rows:]) + 1.0)


def later_pairs(frames, width, reach, sums_ref, sent_ref, got_ref):
    rows = got_ref.shape[0] - 8
    part = got_ref.shape[1]
    tm = lax.axis_index("tm")
    pair, y = tm // 2, tm % 2
    pos = columns((rows, part)) + y * part
    pairs = lax.axis_size("tm") // 2
    got = jnp.where(pair + reach < pairs, unpack(got_ref), 0.0)
    b_cum = sums_ref[4 * jnp.minimum(pair + reach, pairs) + 1]
    b_from, b_next = sums_ref[4 * pair + 1], sums_ref[4 * pair + 5]
    power = jnp.where(pair + reach < pairs, jnp.maximum(sent_ref[rows:], got_ref[rows:]), sent_ref[rows:])
    weight = decay_rate ** (2 * frames * reach)
    weight_next = decay_rate ** (2 * frames * (reach - 1))
    incl = dropped(weight * got, pos, width, b_cum, b_cum - b_from)
    return incl, dropped(weight_next * got, pos, width, b_cum, b_cum - b_next), power


def step_kernel(frames, width, reach, sums_ref, both_ref, sent_ref, got_ref, *refs):
    incl, excl, power = later_pairs(frames, width, reach, sums_ref, sent_ref, got_ref)
    incl_ref, excl_ref, send_ref = refs[-3:]
    both = both_ref[...] + incl
    incl_ref[...] = both
    excl_ref[...] = excl + refs[0][...] if len(refs) == 4 else excl
    pack(send_ref, both, power + 1.0)


def carry_kernel(
    frames, width, reach, sums_ref, wind_in, late_ref, sent_ref, got_ref, z_ref, zgot_ref, *refs
):
    keep_ref, send_ref, wind_ref = refs[-3:]
    rows, part = late_ref.shape
    tm = lax.axis_index("tm")
    pair, y = tm // 2, tm % 2
    _, late, power = later_pairs(frames, width, reach, sums_ref, sent_ref, got_ref)
    if len(refs) == 4:
        late = late + refs[0][...]
    b_from, b_cum = sums_ref[4 * pair + 3], sums_ref[4 * pair + 5]
    pos = columns((rows, part)) + y * part
    moved = dropped(decay_rate**frames * late, pos, width, b_cum, b_cum - b_from)
    early = late_ref[...] + moved
    keep = jnp.where(y == 0, early, late)
    send = jnp.where(y == 0, late, early)
    keep_ref[...] = keep
    pack(send_ref, send, power + 2.0)
    sums = [
        wind_in[i] + jnp.sum(keep * z_ref[i] + send * unpack(zgot_ref.at[i])) for i in range(2)
    ]
    lane = lax.broadcasted_iota(jnp.int32, wind_ref.shape, 2)
    wind_ref[...] = jnp.where(lane == 0, sums[0], jnp.where(lane == 1, sums[1], 0.0))


def final_kernel(sh_ref, sums_ref, keep_ref, got_ref, loc_ref, adj_ref):
    frames, block, width = loc_ref.shape
    rows = keep_ref.shape[0]
    halo = rows - block
    tm = lax.axis_index("tm")
    keep, got = keep_ref[...], unpack(got_ref)
    low = jnp.where(tm % 2 == 0, keep, got)
    high = jnp.where(tm % 2 == 0, got, keep)
    canvas = jnp.concatenate([low, high], axis=1)
    a_cum, b_cum = sums_ref[2 * tm + 2], sums_ref[2 * tm + 3]
    col = columns((block, width))
    b_own = jnp.int32(0)
    for k in reversed(range(frames)):
        a, b = sh_ref[2 * k], sh_ref[2 * k + 1]
        a_cum = a_cum - a
        b_cum = b_cum - b
        b_own = b_own + b
        moved = turned(canvas, rows - halo + a_cum, b_cum)[:block]
        moved = jnp.where(col < width - b_own, decay_rate ** (frames - k) * moved, 0.0)
        adj_ref[k] = loc_ref[k] + moved


def diffs(phases_ref, next_ref, k):
    _, block, width = phases_ref.shape
    here = phases_ref[k].astype(jnp.float32)
    last = next_ref[k : k + 1]
    row = lax.broadcasted_iota(jnp.int32, (block, width), 0)
    below = jnp.where(row == block - 1, last, pltpu.roll(here, block - 1, 0))
    right = jnp.where(columns((block, width)) == width - 1, 0.0, pltpu.roll(here, width - 1, 1))
    return below - here, right - here


def swap(value, axis, bit):
    count = lax.axis_size(axis)
    return lax.ppermute(value, axis, [(s, s ^ bit) for s in range(count)])


def gather_rows(value):
    count = lax.axis_size("rows")
    held = {0: value}
    bit = count // 2
    while bit:
        for d, v in list(held.items()):
            held[d ^ bit] = swap(v, "rows", bit)
        bit //= 2
    return [held[d] for d in range(count)]


def from_later(value, pairs_away):
    count = lax.axis_size("tm")
    route = [(s, s - 2 * pairs_away) for s in range(2 * pairs_away, count)]
    return lax.ppermute(value.astype(jnp.float16), "tm", route).astype(jnp.float32)


def swap_half(value):
    return swap(value.astype(jnp.float16), "tm", 1).astype(jnp.float32)


def kernel_call(body, vmem_mib, out_shape, in_specs, out_specs, cost=0):
    estimate = pl.CostEstimate(flops=0, bytes_accessed=cost, transcendentals=0) if cost else None
    return pl.pallas_call(
        body,
        out_shape=out_shape,
        in_specs=in_specs,
        out_specs=out_specs,
        cost_estimate=estimate,
        compiler_params=pltpu.CompilerParams(vmem_limit_bytes=vmem_mib << 20),
    )


def on_device(phases, focal_data, shifts, pupil_mask):
    frames, block, width = phases.shape
    n_rows = lax.axis_size("rows")
    n_tm = lax.axis_size("tm")
    frames_all = frames * n_tm
    focal = focal_data.shape[3]
    halo = min(frames_all // 2, width // (4 * n_rows))
    halo = -(-halo // 16) * 16
    rows = block + halo
    part = width // 2
    pairs = n_tm // 2
    half = focal // 2
    cs = tables(width, focal)
    tt = np.concatenate([cs.T, np.zeros((halo, 2 * focal), cs.dtype)], axis=0)
    order = np.concatenate([np.arange(half), half + (half - np.arange(half)) % half])
    cs_turned = np.concatenate([cs[order], cs[focal + order]], axis=0)
    y_table = np.concatenate([cs[:half], cs[focal : focal + half]], axis=0).T
    flip = np.zeros((half, half), cs.dtype)
    flip[(half - np.arange(half)) % half, np.arange(half)] = 1
    sh_all = shifts.reshape(2 * frames)
    bit = 1
    while bit < n_tm:
        other = swap(sh_all, "tm", bit)
        sh_all = jnp.concatenate([sh_all, other])
        bit *= 2
    vmem = pl.BlockSpec(memory_space=pltpu.VMEM)
    smem = pl.BlockSpec(memory_space=pltpu.SMEM)
    hbm = pl.BlockSpec(memory_space=pltpu.HBM)
    kept = [tt, cs, cs_turned, flip]
    y, *kept = pl.pallas_call(
        functools.partial(y_kernel, halo),
        out_shape=[
            jax.ShapeDtypeStruct((frames * block + 16 + halo * width // focal, focal), jnp.bfloat16)
        ]
        + [jax.ShapeDtypeStruct(t.shape, jnp.bfloat16) for t in kept],
        in_specs=[hbm] * (3 + len(kept)),
        out_specs=[vmem] * (1 + len(kept)),
        scratch_shapes=[
            pltpu.VMEM(phases.shape, phases.dtype),
            pltpu.VMEM(pupil_mask.shape, pupil_mask.dtype),
            pltpu.VMEM(y_table.shape, y_table.dtype),
            pltpu.SemaphoreType.DMA((3 + len(kept),)),
        ],
        compiler_params=pltpu.CompilerParams(vmem_limit_bytes=8 << 20),
        name="transform",
    )(*[pltpu.with_memory_space_constraint(t, pltpu.HBM) for t in (phases, pupil_mask, y_table, *kept)])
    d_parts = gather_rows(focal_data)
    m_parts = gather_rows(y)
    field = jax.ShapeDtypeStruct((frames, block, width), jnp.float32)
    pair = jax.ShapeDtypeStruct((2,), jnp.float32)
    grads, next_rows = pl.pallas_call(
        functools.partial(grad_kernel, n_rows, halo),
        out_shape=(
            jax.ShapeDtypeStruct((frames, rows, width), jnp.float32),
            jax.ShapeDtypeStruct((-(-frames // 8) * 8, width), jnp.float32),
        ),
        in_specs=[vmem] * (2 * n_rows + 5),
        out_specs=(vmem, vmem),
        scratch_shapes=[
            pltpu.VMEM((frames, width, focal), jnp.bfloat16),
            pltpu.VMEM((16, width), jnp.bfloat16),
            pltpu.VMEM((frames, 2, focal, focal), jnp.bfloat16),
            pltpu.VMEM((2 * focal, 2 * focal), jnp.bfloat16),
            pltpu.VMEM((frames, rows, 2 * focal), jnp.bfloat16),
            pltpu.VMEM((halo, width), jnp.float32),
        ],
        compiler_params=pltpu.CompilerParams(vmem_limit_bytes=24 << 20),
        name="grad",
    )(*m_parts, *d_parts, pupil_mask, *kept)
    half_field = jax.ShapeDtypeStruct((rows, part), jnp.float32)
    message = jax.ShapeDtypeStruct((rows + 8, part), jnp.float32)
    loc, keep, send, sums_all = kernel_call(
        segment_kernel, 12,
        (field, half_field, message, jax.ShapeDtypeStruct((2 * n_tm + 2,), jnp.int32)),
        [smem, vmem], (vmem, vmem, vmem, smem),
    )(sh_all, grads)
    late, both, send = kernel_call(
        functools.partial(combine_kernel, frames, width), 6,
        (half_field, half_field, message), [smem] + [vmem] * 3, (vmem, vmem, vmem),
    )(sums_all, keep, send, swap_half(send))
    z_keep, z_send, wind_local = kernel_call(
        functools.partial(z_kernel, halo), 12,
        (
            jax.ShapeDtypeStruct((2, rows, part), jnp.float32),
            jax.ShapeDtypeStruct((2, rows + 8, part), jnp.float32),
            pair,
        ),
        [smem, smem] + [vmem] * 4 + [pl.BlockSpec(memory_space=pl.ANY)], (vmem, vmem, smem),
    )(sh_all, sums_all, phases, next_rows, grads, loc, late)
    z_got = swap_half(z_send)
    sums = []
    reach = 1
    while 2 * reach < pairs:
        both, excl, send = kernel_call(
            functools.partial(step_kernel, frames, width, reach), 6,
            (half_field, half_field, message),
            [smem] + [vmem] * (3 + len(sums)), (vmem, vmem, vmem),
        )(sums_all, both, send, from_later(send, reach), *sums)
        sums = [excl]
        reach *= 2
    n_all = n_tm * n_rows
    keep, send, wind = kernel_call(
        functools.partial(carry_kernel, frames, width, reach), 8,
        (half_field, message, jax.ShapeDtypeStruct((n_all, 1, LANES), jnp.float32)),
        [smem, smem] + [vmem] * (5 + len(sums)), (vmem, vmem, vmem),
    )(sums_all, wind_local, late, send, from_later(send, reach), z_keep, z_got, *sums)
    winds = lax.all_to_all(wind, ("tm", "rows"), 0, 0)
    got = swap_half(send)
    adjoint = kernel_call(
        final_kernel, 8, field, [smem, smem, vmem, vmem, vmem], vmem,
        cost=12 * frames * block * width,
    )(sh_all, sums_all, keep, got, loc)
    wind_grad = -jnp.sum(winds[:, 0, :2], axis=0) / (width * frames_all)
    return adjoint, wind_grad


def solution(mesh):
    in_specs = (P("tm", "rows", None), P("tm", None, "rows", None), P("tm", None), P("rows", None))
    out_specs = (P("tm", "rows", None), P())

    return jax.shard_map(
        on_device, mesh=mesh, in_specs=in_specs, out_specs=out_specs, check_vma=False
    )
```

```python
import functools
import math

import jax
import jax.numpy as jnp
import numpy as np
from jax import lax
from jax.experimental import pallas as pl
from jax.experimental.pallas import tpu as pltpu
from jax.sharding import PartitionSpec as P

decay_rate = 0.999
LANES = 128


def tables(pupil, focal):
    focal_pos = np.arange(focal) - focal // 2
    pupil_pos = np.arange(pupil) - pupil // 2
    turns = np.mod(focal_pos[:, None] * pupil_pos[None, :], 2 * pupil)
    angle = turns.astype(np.float32) * np.float32(math.pi / pupil)
    factor = np.float32(1.0 / math.sqrt(pupil))
    cos_t = (np.cos(angle) * factor).astype(jnp.bfloat16)
    sin_t = (-np.sin(angle) * factor).astype(jnp.bfloat16)
    return np.concatenate([cos_t, sin_t], axis=0)


def dot(a, b):
    return jnp.dot(a, b, preferred_element_type=jnp.float32)


def turned(value, down, right):
    value = pltpu.roll(value, lax.rem(down, value.shape[0]), 0)
    return pltpu.roll(value, lax.rem(right, value.shape[1]), 1)


def columns(shape):
    return lax.broadcasted_iota(jnp.int32, shape, 1)


def y_kernel(halo, phases_hbm, mask_hbm, half_hbm, *refs):
    count = (len(refs) - 5) // 2
    y_ref = refs[count]
    phases_ref, mask_ref, half_ref, sem = refs[-4:]
    ins = [(phases_hbm, phases_ref), (mask_hbm, mask_ref), (half_hbm, half_ref)]
    copies = [(refs[i], refs[count + 1 + i]) for i in range(count)]
    copies = [
        pltpu.make_async_copy(src, dst, sem.at[i]) for i, (src, dst) in enumerate(ins + copies)
    ]
    for copy in copies:
        copy.start()
    for copy in copies[:3]:
        copy.wait()
    frames, block, width = phases_ref.shape
    focal = y_ref.shape[1]
    parts = width // focal
    live = mask_ref[...] == 1
    zero_freq = jnp.full((16, width), zero_freq_value(width), jnp.bfloat16)
    row = lax.broadcasted_iota(jnp.int32, (16, block), 0)
    rows = lax.broadcasted_iota(jnp.int32, (16, focal), 0)
    dc = jnp.zeros((16, block), jnp.float32)
    edge = jnp.zeros((16, focal), jnp.float32)
    for k in range(frames):
        masked = jnp.where(live, phases_ref[k].astype(jnp.float32), 0.0).astype(jnp.bfloat16)
        y_ref[k * block : (k + 1) * block] = dot(masked, half_ref[...]).astype(jnp.bfloat16)
        dc = jnp.where(row == k, dot_t(zero_freq, masked), dc)
        top = phases_ref[k, :8].astype(jnp.float32)[:1]
        for i in range(parts):
            here = jnp.broadcast_to(top[:, i * focal : (i + 1) * focal], edge.shape)
            edge = jnp.where(rows == frames + k * parts + i, here, edge)
    at = frames * block
    y_ref[at : at + 16] = edge.astype(jnp.bfloat16)
    y_ref[at : at + 16, :block] = (edge[:, :block] + dc).astype(jnp.bfloat16)
    at = at + 16
    mask = mask_ref[:halo].astype(jnp.float32).astype(jnp.bfloat16)
    for i in range(parts):
        y_ref[at + i * halo : at + (i + 1) * halo] = mask[:, i * focal : (i + 1) * focal]
    for copy in copies[3:]:
        copy.wait()


def zero_freq_value(width):
    return float(np.float32(np.float32(1.0 / math.sqrt(width)).astype(jnp.bfloat16)))


def dot_t(a, b):
    return lax.dot_general(a, b, (((1,), (1,)), ((), ())), preferred_element_type=jnp.float32)


def grad_kernel(n_rows, halo, *refs):
    m_refs, d_refs = refs[:n_rows], refs[n_rows : 2 * n_rows]
    mask_ref, tt_ref, cs_ref, turned_ref, flip_ref = refs[2 * n_rows : 2 * n_rows + 5]
    g_ref, next_ref = refs[2 * n_rows + 5 : 2 * n_rows + 7]
    y_ref, dc_ref, d_ref, r_ref, w_ref, over_ref = refs[2 * n_rows + 7 :]
    frames = w_ref.shape[0]
    block, width = mask_ref.shape
    focal = cs_ref.shape[0] // 2
    parts = width // focal
    half = focal // 2
    part = focal // n_rows
    rows = block + halo
    me = lax.axis_index("rows")
    over_ref[...] = jnp.zeros_like(over_ref)
    next_ref[...] = jnp.zeros_like(next_ref)
    for d in range(1, n_rows):

        @pl.when((me ^ d) == me + 1)
        def _():
            at = frames * block
            edge = m_refs[d][at : at + 16].astype(jnp.float32)
            for k in range(frames):
                for i in range(parts):
                    line = frames + k * parts + i
                    next_ref[k : k + 1, i * focal : (i + 1) * focal] = edge[line : line + 1]
            at = at + 16
            for i in range(parts):
                over_ref[:, i * focal : (i + 1) * focal] = m_refs[d][
                    at + i * halo : at + (i + 1) * halo
                ].astype(jnp.float32)

    for d in range(n_rows):
        at = pl.multiple_of((me ^ d) * block, block)
        at_q = pl.multiple_of((me ^ d) * part, part)
        for k in range(frames):
            y_ref[k, pl.ds(at, block), :] = m_refs[d][k * block : (k + 1) * block]
            d_ref[k, :, pl.ds(at_q, part), :] = d_refs[d][k]
        dc_ref[:, pl.ds(at, block)] = m_refs[d][frames * block : frames * block + 16, :block]
    dc = dot_t(cs_ref[...], dc_ref[...])
    first = columns((focal, half)) == 0
    for k in range(frames):
        pq = dot(cs_ref[...], y_ref[k])
        c_real, c_imag = pq[:focal, :half], pq[:focal, half:]
        s_real, s_imag = pq[focal:, :half], pq[focal:, half:]
        e_real = (c_real - s_imag, jnp.where(first, dc[:focal, k : k + 1], c_real + s_imag))
        e_imag = (c_imag + s_real, jnp.where(first, dc[focal:, k : k + 1], s_real - c_imag))
        for i in range(2):
            at = slice(i * half, (i + 1) * half)
            real, imag = d_ref[k, 0, :, at], d_ref[k, 1, :, at]
            if i:
                real, imag = dot(real, flip_ref[...]), dot(imag, flip_ref[...])
            real = (real.astype(jnp.float32) - e_real[i]).astype(jnp.bfloat16)
            imag = (imag.astype(jnp.float32) - e_imag[i]).astype(jnp.bfloat16)
            r_ref[:focal, i * half : (i + 1) * half] = real
            r_ref[:focal, focal + i * half : focal + (i + 1) * half] = imag
            r_ref[focal:, i * half : (i + 1) * half] = imag
            r_ref[focal:, focal + i * half : focal + (i + 1) * half] = -real
        rows_t = tt_ref[pl.ds(pl.multiple_of(me * block, block), rows), :]
        w_ref[k] = dot(rows_t, r_ref[...]).astype(jnp.bfloat16)
    live = mask_ref[...] == 1
    live_over = over_ref[...] == 1.0
    for k in range(frames):
        g = dot(w_ref[k], turned_ref[...])
        g_ref[k, :block] = jnp.where(live, g[:block], 0.0)
        g_ref[k, block:] = jnp.where(live_over, g[block:], 0.0)


def halves(value, rows, start, y):
    low, high = value[:rows], value[start : start + rows]
    return jnp.where(y == 0, low, high), jnp.where(y == 0, high, low)


def back(value, down, right):
    rows, width = value.shape
    row = lax.broadcasted_iota(jnp.int32, value.shape, 0)
    inside = (columns(value.shape) < width - right) & (row < rows - down)
    return jnp.where(inside, turned(value, rows - down, width - right), 0.0)


def own_shifts(sh_ref, first, stop):
    down, right = jnp.int32(0), jnp.int32(0)
    for k in range(first, stop):
        down, right = down + sh_ref[2 * k], right + sh_ref[2 * k + 1]
    return down, right


def exponent(value, width):
    top = jnp.full((8, width), jnp.maximum(jnp.max(jnp.abs(value)), 1e-30))
    return jnp.ceil(jnp.log2(top))[:1]


def pack(ref, value, power, down=0, right=0):
    rows = value.shape[0]
    ref[:rows] = value * jnp.exp2(-power)
    line = lax.broadcasted_iota(jnp.int32, (8, value.shape[1]), 0)
    shift = jnp.where(line == 1, down, right).astype(jnp.float32)
    ref[rows:] = jnp.where(line == 0, power, shift)


def power_of(ref):
    rows = ref.shape[0] - 8
    return ref[rows : rows + 1]


def shift_of(ref):
    rows = ref.shape[0] - 8
    return ref[rows + 1, 0].astype(jnp.int32), ref[rows + 2, 0].astype(jnp.int32)


def unpack(ref):
    return ref[: ref.shape[0] - 8] * jnp.exp2(power_of(ref))


def segment_kernel(sh_ref, g_ref, loc_ref, keep_ref, send_ref):
    frames, block, _ = loc_ref.shape
    lam = g_ref[frames - 1]
    loc_ref[frames - 1] = lam[:block]
    for k in reversed(range(frames - 1)):
        lam = g_ref[k] + decay_rate * back(lam, sh_ref[2 * k], sh_ref[2 * k + 1])
        loc_ref[k] = lam[:block]
    keep, send = halves(lam, keep_ref.shape[0], block // 2, lax.axis_index("tm") % 2)
    keep_ref[...] = keep
    pack(send_ref, send, exponent(lam, lam.shape[1]), *own_shifts(sh_ref, 0, frames))


def z_kernel(
    sh_ref, phases_ref, next_ref, g_ref, loc_ref, after_ref, keep_ref, send_ref, wind_ref
):
    frames, block, width = phases_ref.shape
    part = keep_ref.shape[1]
    rows = block // 2 + part
    pad = jnp.zeros((rows - block, width), jnp.float32)
    col = columns((rows, width))
    row = lax.broadcasted_iota(jnp.int32, (part, width), 0)
    sums = [jnp.zeros((rows, width), jnp.float32) for _ in range(2)]
    winds = [jnp.float32(0.0), jnp.float32(0.0)]
    for k in reversed(range(frames)):
        down, right = own_shifts(sh_ref, k, frames)
        for i, diff in enumerate(diffs(phases_ref, next_ref, k)):
            if k < frames - 1:
                winds[i] = winds[i] + jnp.sum((loc_ref[k] - g_ref[k, :block]) * diff)
            diff = jnp.concatenate([decay_rate ** (frames - k) * diff, pad], axis=0)
            sums[i] = sums[i] + jnp.where(col >= right, turned(diff, down, right), 0.0)
    y = lax.axis_index("tm") % 2
    for i in range(2):
        low = jnp.where(row < block // 2, sums[i][:part], 0.0)
        high = sums[i][block // 2 :]
        keep_ref[i] = jnp.where(y == 0, low, high)
        send = jnp.where(y == 0, high, low)
        pack(send_ref.at[i], send, exponent(send, width))
        wind_ref[i] = winds[i]


def combine_kernel(
    frames, sh_ref, keep_ref, sent_ref, got_ref, late_ref, both_ref, send_ref, info_ref
):
    y = lax.axis_index("tm") % 2
    keep, got = keep_ref[...], unpack(got_ref)
    early = jnp.where(y == 0, keep, got)
    late = jnp.where(y == 0, got, keep)
    late_ref[...] = late
    own = own_shifts(sh_ref, 0, frames)
    other = shift_of(got_ref)
    first = [jnp.where(y == 0, own[i], other[i]) for i in range(2)]
    total = [own[i] + other[i] for i in range(2)]
    for i in range(2):
        info_ref[i] = total[i] - first[i]
        info_ref[2 + i] = total[i]
    both = early + decay_rate**frames * back(late, *first)
    both_ref[...] = both
    pack(send_ref, both, jnp.maximum(power_of(sent_ref), power_of(got_ref)) + 1.0, *total)


def from_pairs(reach, sent_ref, got_ref):
    pair = lax.axis_index("tm") // 2
    there = pair + reach < lax.axis_size("tm") // 2
    power = power_of(sent_ref)
    power = jnp.where(there, jnp.maximum(power, power_of(got_ref)), power)
    return jnp.where(there, unpack(got_ref), 0.0), power


def step_kernel(frames, reach, info_ref, both_ref, sent_ref, got_ref, *refs):
    incl_ref, excl_ref, send_ref = refs[-3:]
    got, power = from_pairs(reach, sent_ref, got_ref)
    span, more = shift_of(sent_ref), shift_of(got_ref)
    both = both_ref[...] + decay_rate ** (2 * frames * reach) * back(got, *span)
    incl_ref[...] = both
    if reach == 1:
        excl_ref[...] = got
    else:
        apart = [span[i] - info_ref[2 + i] for i in range(2)]
        excl_ref[...] = refs[0][...] + decay_rate ** (2 * frames * (reach - 1)) * back(got, *apart)
    pack(send_ref, both, power + 1.0, span[0] + more[0], span[1] + more[1])


def carry_kernel(
    frames, reach, info_ref, wind_in, late_ref, sent_ref, got_ref, z_ref, zgot_ref, *refs
):
    keep_ref, send_ref, wind_ref = refs[-3:]
    y = lax.axis_index("tm") % 2
    late, power = from_pairs(reach, sent_ref, got_ref)
    if reach > 1:
        span = shift_of(sent_ref)
        apart = [span[i] - info_ref[2 + i] for i in range(2)]
        late = refs[0][...] + decay_rate ** (2 * frames * (reach - 1)) * back(late, *apart)
    early = late_ref[...] + decay_rate**frames * back(late, info_ref[0], info_ref[1])
    keep = jnp.where(y == 0, early, late)
    send = jnp.where(y == 0, late, early)
    keep_ref[...] = keep
    pack(send_ref, send, power + 2.0)
    sums = [
        wind_in[i] + jnp.sum(keep * z_ref[i] + send * unpack(zgot_ref.at[i])) for i in range(2)
    ]
    lane = lax.broadcasted_iota(jnp.int32, wind_ref.shape, 2)
    wind_ref[...] = jnp.where(lane == 0, sums[0], jnp.where(lane == 1, sums[1], 0.0))


def final_kernel(sh_ref, keep_ref, got_ref, loc_ref, adj_ref):
    frames, block, _ = loc_ref.shape
    y = lax.axis_index("tm") % 2
    keep, got = keep_ref[...], unpack(got_ref)
    low = jnp.where(y == 0, keep, got)
    high = jnp.where(y == 0, got, keep)
    field = jnp.concatenate([low[: block // 2], high], axis=0)
    for k in reversed(range(frames)):
        moved = back(field, *own_shifts(sh_ref, k, frames))[:block]
        adj_ref[k] = loc_ref[k] + decay_rate ** (frames - k) * moved


def diffs(phases_ref, next_ref, k):
    _, block, width = phases_ref.shape
    here = phases_ref[k].astype(jnp.float32)
    last = next_ref[k : k + 1]
    row = lax.broadcasted_iota(jnp.int32, (block, width), 0)
    below = jnp.where(row == block - 1, last, pltpu.roll(here, block - 1, 0))
    right = jnp.where(columns((block, width)) == width - 1, 0.0, pltpu.roll(here, width - 1, 1))
    return below - here, right - here


def swap(value, axis, bit):
    count = lax.axis_size(axis)
    return lax.ppermute(value, axis, [(s, s ^ bit) for s in range(count)])


def gather_rows(value):
    count = lax.axis_size("rows")
    held = {0: value}
    bit = count // 2
    while bit:
        for d, v in list(held.items()):
            held[d ^ bit] = swap(v, "rows", bit)
        bit //= 2
    return [held[d] for d in range(count)]


def from_later(value, pairs_away):
    count = lax.axis_size("tm")
    route = [(s, s - 2 * pairs_away) for s in range(2 * pairs_away, count)]
    return lax.ppermute(value.astype(jnp.float16), "tm", route).astype(jnp.float32)


def swap_half(value):
    return swap(value.astype(jnp.float16), "tm", 1).astype(jnp.float32)


def kernel_call(body, vmem_mib, out_shape, in_specs, out_specs, cost=0):
    estimate = pl.CostEstimate(flops=0, bytes_accessed=cost, transcendentals=0) if cost else None
    return pl.pallas_call(
        body,
        out_shape=out_shape,
        in_specs=in_specs,
        out_specs=out_specs,
        cost_estimate=estimate,
        compiler_params=pltpu.CompilerParams(vmem_limit_bytes=vmem_mib << 20),
    )


def on_device(phases, focal_data, shifts, pupil_mask):
    frames, block, width = phases.shape
    n_rows = lax.axis_size("rows")
    n_tm = lax.axis_size("tm")
    frames_all = frames * n_tm
    focal = focal_data.shape[3]
    reach_rows = -(-min(frames_all // 2, width // (4 * n_rows)) // 8) * 8
    halo = -(-reach_rows // 16) * 16
    rows = block + halo
    part = block // 2 + reach_rows
    pairs = n_tm // 2
    half = focal // 2
    cs = tables(width, focal)
    tt = np.concatenate([cs.T, np.zeros((halo, 2 * focal), cs.dtype)], axis=0)
    order = np.concatenate([np.arange(half), half + (half - np.arange(half)) % half])
    cs_turned = np.concatenate([cs[order], cs[focal + order]], axis=0)
    y_table = np.concatenate([cs[:half], cs[focal : focal + half]], axis=0).T
    flip = np.zeros((half, half), cs.dtype)
    flip[(half - np.arange(half)) % half, np.arange(half)] = 1
    own = shifts.reshape(2 * frames)
    vmem = pl.BlockSpec(memory_space=pltpu.VMEM)
    smem = pl.BlockSpec(memory_space=pltpu.SMEM)
    hbm = pl.BlockSpec(memory_space=pltpu.HBM)
    kept = [tt, cs, cs_turned, flip]
    y, *kept = pl.pallas_call(
        functools.partial(y_kernel, halo),
        out_shape=[
            jax.ShapeDtypeStruct((frames * block + 16 + halo * width // focal, focal), jnp.bfloat16)
        ]
        + [jax.ShapeDtypeStruct(t.shape, jnp.bfloat16) for t in kept],
        in_specs=[hbm] * (3 + len(kept)),
        out_specs=[vmem] * (1 + len(kept)),
        scratch_shapes=[
            pltpu.VMEM(phases.shape, phases.dtype),
            pltpu.VMEM(pupil_mask.shape, pupil_mask.dtype),
            pltpu.VMEM(y_table.shape, y_table.dtype),
            pltpu.SemaphoreType.DMA((3 + len(kept),)),
        ],
        compiler_params=pltpu.CompilerParams(vmem_limit_bytes=8 << 20),
        name="transform",
    )(*[pltpu.with_memory_space_constraint(t, pltpu.HBM) for t in (phases, pupil_mask, y_table, *kept)])
    d_parts = gather_rows(focal_data)
    m_parts = gather_rows(y)
    field = jax.ShapeDtypeStruct((frames, block, width), jnp.float32)
    pair = jax.ShapeDtypeStruct((2,), jnp.float32)
    grads, next_rows = pl.pallas_call(
        functools.partial(grad_kernel, n_rows, halo),
        out_shape=(
            jax.ShapeDtypeStruct((frames, rows, width), jnp.float32),
            jax.ShapeDtypeStruct((-(-frames // 8) * 8, width), jnp.float32),
        ),
        in_specs=[vmem] * (2 * n_rows + 5),
        out_specs=(vmem, vmem),
        scratch_shapes=[
            pltpu.VMEM((frames, width, focal), jnp.bfloat16),
            pltpu.VMEM((16, width), jnp.bfloat16),
            pltpu.VMEM((frames, 2, focal, focal), jnp.bfloat16),
            pltpu.VMEM((2 * focal, 2 * focal), jnp.bfloat16),
            pltpu.VMEM((frames, rows, 2 * focal), jnp.bfloat16),
            pltpu.VMEM((halo, width), jnp.float32),
        ],
        compiler_params=pltpu.CompilerParams(vmem_limit_bytes=24 << 20),
        name="grad",
    )(*m_parts, *d_parts, pupil_mask, *kept)
    half_field = jax.ShapeDtypeStruct((part, width), jnp.float32)
    message = jax.ShapeDtypeStruct((part + 8, width), jnp.float32)
    loc, keep, send = kernel_call(
        segment_kernel, 12, (field, half_field, message), [smem, vmem], (vmem,) * 3
    )(own, grads)
    late, both, send, info = kernel_call(
        functools.partial(combine_kernel, frames), 6,
        (half_field, half_field, message, jax.ShapeDtypeStruct((4,), jnp.int32)),
        [smem] + [vmem] * 3, (vmem, vmem, vmem, smem),
    )(own, keep, send, swap_half(send))
    z_keep, z_send, wind_local = kernel_call(
        z_kernel, 12,
        (
            jax.ShapeDtypeStruct((2, part, width), jnp.float32),
            jax.ShapeDtypeStruct((2, part + 8, width), jnp.float32),
            pair,
        ),
        [smem] + [vmem] * 4 + [pl.BlockSpec(memory_space=pl.ANY)], (vmem, vmem, smem),
    )(own, phases, next_rows, grads, loc, late)
    z_got = swap_half(z_send)
    sums = []
    reach = 1
    while 2 * reach < pairs:
        both, excl, send = kernel_call(
            functools.partial(step_kernel, frames, reach), 6,
            (half_field, half_field, message),
            [smem] + [vmem] * (3 + len(sums)), (vmem, vmem, vmem),
        )(info, both, send, from_later(send, reach), *sums)
        sums = [excl]
        reach *= 2
    n_all = n_tm * n_rows
    keep, send, wind = kernel_call(
        functools.partial(carry_kernel, frames, reach), 8,
        (half_field, message, jax.ShapeDtypeStruct((n_all, 1, LANES), jnp.float32)),
        [smem, smem] + [vmem] * (5 + len(sums)), (vmem, vmem, vmem),
    )(info, wind_local, late, send, from_later(send, reach), z_keep, z_got, *sums)
    winds = lax.all_to_all(wind, ("tm", "rows"), 0, 0)
    got = swap_half(send)
    adjoint = kernel_call(
        final_kernel, 8, field, [smem, vmem, vmem, vmem], vmem,
        cost=12 * frames * block * width,
    )(own, keep, got, loc)
    wind_grad = -jnp.sum(winds[:, 0, :2], axis=0) / (width * frames_all)
    return adjoint, wind_grad


def solution(mesh):
    in_specs = (P("tm", "rows", None), P("tm", None, "rows", None), P("tm", None), P("rows", None))
    out_specs = (P("tm", "rows", None), P())

    return jax.shard_map(
        on_device, mesh=mesh, in_specs=in_specs, out_specs=out_specs, check_vma=False
    )
```

```python
import functools
import math

import jax
import jax.numpy as jnp
import numpy as np
from jax import lax
from jax.experimental import pallas as pl
from jax.experimental.pallas import tpu as pltpu
from jax.sharding import PartitionSpec as P

decay_rate = 0.999
LANES = 128


def tables(pupil, focal):
    focal_pos = np.arange(focal) - focal // 2
    pupil_pos = np.arange(pupil) - pupil // 2
    turns = np.mod(focal_pos[:, None] * pupil_pos[None, :], 2 * pupil)
    angle = turns.astype(np.float32) * np.float32(math.pi / pupil)
    factor = np.float32(1.0 / math.sqrt(pupil))
    cos_t = (np.cos(angle) * factor).astype(jnp.bfloat16)
    sin_t = (-np.sin(angle) * factor).astype(jnp.bfloat16)
    return np.concatenate([cos_t, sin_t], axis=0)


def dot(a, b):
    return jnp.dot(a, b, preferred_element_type=jnp.float32)


def turned(value, down, right):
    value = pltpu.roll(value, lax.rem(down, value.shape[0]), 0)
    return pltpu.roll(value, lax.rem(right, value.shape[1]), 1)


def columns(shape):
    return lax.broadcasted_iota(jnp.int32, shape, 1)


def y_kernel(halo, phases_hbm, mask_hbm, half_hbm, *refs):
    count = (len(refs) - 6) // 2
    y_ref, side_ref = refs[count], refs[-5]
    phases_ref, mask_ref, half_ref, sem = refs[-4:]
    ins = [(phases_hbm, phases_ref), (mask_hbm, mask_ref), (half_hbm, half_ref)]
    copies = [(refs[i], refs[count + 1 + i]) for i in range(count)]
    copies = [
        pltpu.make_async_copy(src, dst, sem.at[i]) for i, (src, dst) in enumerate(ins + copies)
    ]
    for copy in copies:
        copy.start()
    for copy in copies[:3]:
        copy.wait()
    frames, block, width = phases_ref.shape
    focal = y_ref.shape[1]
    parts = width // focal
    live = mask_ref[...] == 1
    zero_freq = jnp.full((16, width), zero_freq_value(width), jnp.bfloat16)
    row = lax.broadcasted_iota(jnp.int32, (16, block), 0)
    rows = lax.broadcasted_iota(jnp.int32, (16, focal), 0)
    dc = jnp.zeros((16, block), jnp.float32)
    edge = jnp.zeros((16, focal), jnp.float32)
    for k in range(frames):
        masked = jnp.where(live, phases_ref[k].astype(jnp.float32), 0.0).astype(jnp.bfloat16)
        y_ref[k * block : (k + 1) * block] = dot(masked, half_ref[...]).astype(jnp.bfloat16)
        dc = jnp.where(row == k, dot_t(zero_freq, masked), dc)
        top = phases_ref[k, :8].astype(jnp.float32)[:1]
        for i in range(parts):
            here = jnp.broadcast_to(top[:, i * focal : (i + 1) * focal], edge.shape)
            edge = jnp.where(rows == frames + k * parts + i, here, edge)
    at = frames * block
    y_ref[at : at + 16] = edge.astype(jnp.bfloat16)
    y_ref[at : at + 16, :block] = (edge[:, :block] + dc).astype(jnp.bfloat16)
    at = at + 16
    mask = mask_ref[:halo].astype(jnp.float32).astype(jnp.bfloat16)
    for i in range(parts):
        y_ref[at + i * halo : at + (i + 1) * halo] = mask[:, i * focal : (i + 1) * focal]
    side_ref[...] = half_phases(phases_ref, 1 - lax.axis_index("tm") % 2)
    for copy in copies[3:]:
        copy.wait()


def half_phases(phases_ref, y):
    block = phases_ref.shape[1]
    part = block // 2 + 8
    low = phases_ref[:, :part].astype(jnp.float32)
    high = phases_ref[:, block - part :].astype(jnp.float32)
    return jnp.where(y == 0, low, high).astype(jnp.bfloat16)


def zero_freq_value(width):
    return float(np.float32(np.float32(1.0 / math.sqrt(width)).astype(jnp.bfloat16)))


def dot_t(a, b):
    return lax.dot_general(a, b, (((1,), (1,)), ((), ())), preferred_element_type=jnp.float32)


def grad_kernel(n_rows, halo, *refs):
    m_refs, d_refs = refs[:n_rows], refs[n_rows : 2 * n_rows]
    mask_ref, tt_ref, cs_ref, turned_ref, flip_ref = refs[2 * n_rows : 2 * n_rows + 5]
    g_ref, next_ref = refs[2 * n_rows + 5 : 2 * n_rows + 7]
    y_ref, dc_ref, d_ref, r_ref, w_ref, over_ref = refs[2 * n_rows + 7 :]
    frames = w_ref.shape[0]
    block, width = mask_ref.shape
    focal = cs_ref.shape[0] // 2
    parts = width // focal
    half = focal // 2
    part = focal // n_rows
    rows = block + halo
    me = lax.axis_index("rows")
    over_ref[...] = jnp.zeros_like(over_ref)
    next_ref[...] = jnp.zeros_like(next_ref)
    for d in range(1, n_rows):

        @pl.when((me ^ d) == me + 1)
        def _():
            at = frames * block
            edge = m_refs[d][at : at + 16].astype(jnp.float32)
            for k in range(frames):
                for i in range(parts):
                    line = frames + k * parts + i
                    next_ref[k : k + 1, i * focal : (i + 1) * focal] = edge[line : line + 1]
            at = at + 16
            for i in range(parts):
                over_ref[:, i * focal : (i + 1) * focal] = m_refs[d][
                    at + i * halo : at + (i + 1) * halo
                ].astype(jnp.float32)

    for d in range(n_rows):
        at = pl.multiple_of((me ^ d) * block, block)
        at_q = pl.multiple_of((me ^ d) * part, part)
        for k in range(frames):
            y_ref[k, pl.ds(at, block), :] = m_refs[d][k * block : (k + 1) * block]
            d_ref[k, :, pl.ds(at_q, part), :] = d_refs[d][k]
        dc_ref[:, pl.ds(at, block)] = m_refs[d][frames * block : frames * block + 16, :block]
    dc = dot_t(cs_ref[...], dc_ref[...])
    first = columns((focal, half)) == 0
    for k in range(frames):
        pq = dot(cs_ref[...], y_ref[k])
        c_real, c_imag = pq[:focal, :half], pq[:focal, half:]
        s_real, s_imag = pq[focal:, :half], pq[focal:, half:]
        e_real = (c_real - s_imag, jnp.where(first, dc[:focal, k : k + 1], c_real + s_imag))
        e_imag = (c_imag + s_real, jnp.where(first, dc[focal:, k : k + 1], s_real - c_imag))
        for i in range(2):
            at = slice(i * half, (i + 1) * half)
            real, imag = d_ref[k, 0, :, at], d_ref[k, 1, :, at]
            if i:
                real, imag = dot(real, flip_ref[...]), dot(imag, flip_ref[...])
            real = (real.astype(jnp.float32) - e_real[i]).astype(jnp.bfloat16)
            imag = (imag.astype(jnp.float32) - e_imag[i]).astype(jnp.bfloat16)
            r_ref[:focal, i * half : (i + 1) * half] = real
            r_ref[:focal, focal + i * half : focal + (i + 1) * half] = imag
            r_ref[focal:, i * half : (i + 1) * half] = imag
            r_ref[focal:, focal + i * half : focal + (i + 1) * half] = -real
        rows_t = tt_ref[pl.ds(pl.multiple_of(me * block, block), rows), :]
        w_ref[k] = dot(rows_t, r_ref[...]).astype(jnp.bfloat16)
    live = mask_ref[...] == 1
    live_over = over_ref[...] == 1.0
    for k in range(frames):
        g = dot(w_ref[k], turned_ref[...])
        g_ref[k, :block] = jnp.where(live, g[:block], 0.0)
        g_ref[k, block:] = jnp.where(live_over, g[block:], 0.0)


def halves(value, rows, start, y):
    low, high = value[:rows], value[start : start + rows]
    return jnp.where(y == 0, low, high), jnp.where(y == 0, high, low)


def back(value, down, right):
    rows, width = value.shape
    row = lax.broadcasted_iota(jnp.int32, value.shape, 0)
    inside = (columns(value.shape) < width - right) & (row < rows - down)
    return jnp.where(inside, turned(value, rows - down, width - right), 0.0)


def own_shifts(sh_ref, first, stop):
    down, right = jnp.int32(0), jnp.int32(0)
    for k in range(first, stop):
        down, right = down + sh_ref[2 * k], right + sh_ref[2 * k + 1]
    return down, right


def exponent(value, width):
    top = jnp.full((8, width), jnp.maximum(jnp.max(jnp.abs(value)), 1e-30))
    return jnp.ceil(jnp.log2(top))[:1]


def pack(ref, value, power, down=0, right=0, more=()):
    rows = value.shape[0]
    ref[:rows] = value * jnp.exp2(-power)
    line = lax.broadcasted_iota(jnp.int32, (8, value.shape[1]), 0)
    shift = jnp.where(line == 1, down, right).astype(jnp.float32)
    tail = jnp.where(line == 0, power, shift)
    for i, extra in enumerate(more):
        tail = jnp.where(line == 3 + i, extra, tail)
    ref[rows:] = tail


def power_of(ref):
    rows = ref.shape[0] - 8
    return ref[rows : rows + 1]


def shift_of(ref):
    rows = ref.shape[0] - 8
    return ref[rows + 1, 0].astype(jnp.int32), ref[rows + 2, 0].astype(jnp.int32)


def unpack(ref):
    return ref[: ref.shape[0] - 8] * jnp.exp2(power_of(ref))


def segment_kernel(sh_ref, g_ref, next_ref, loc_ref, keep_ref, send_keep_ref, send_ref):
    frames, block, _ = loc_ref.shape
    lam = g_ref[frames - 1]
    loc_ref[frames - 1] = lam[:block]
    for k in reversed(range(frames - 1)):
        lam = g_ref[k] + decay_rate * back(lam, sh_ref[2 * k], sh_ref[2 * k + 1])
        loc_ref[k] = lam[:block]
    keep, send = halves(lam, keep_ref.shape[0], block // 2, lax.axis_index("tm") % 2)
    keep_ref[...] = keep
    power = exponent(lam, lam.shape[1])
    shift = own_shifts(sh_ref, 0, frames)
    pack(send_keep_ref, keep, power, *shift)
    each = jnp.zeros((1, lam.shape[1]), jnp.float32)
    lane = columns(each.shape)
    for i in range(2 * frames):
        each = jnp.where(lane == i, sh_ref[i].astype(jnp.float32), each)
    more = [next_ref[k : k + 1] for k in range(frames)] + [each]
    pack(send_ref, send, power, *shift, more)


def half_diffs(here, last):
    rows, width = here.shape
    row = lax.broadcasted_iota(jnp.int32, here.shape, 0)
    below = jnp.where(row == rows - 1, last, pltpu.roll(here, rows - 1, 0))
    right = jnp.where(columns(here.shape) == width - 1, 0.0, pltpu.roll(here, width - 1, 1))
    return below - here, right - here


def half_products(side, lasts, shifts, y, rows):
    frames, part, width = side.shape
    half = part - 8
    line = lax.broadcasted_iota(jnp.int32, (part, width), 0)
    col = columns((part, width))
    sums = [jnp.zeros((part, width), jnp.float32) for _ in range(2)]
    down, right = jnp.int32(0), jnp.int32(0)
    for k in reversed(range(frames)):
        down, right = down + shifts[k][0], right + shifts[k][1]
        low = jnp.where(y == 0, down, 0)
        high = jnp.where(y == 0, half, half + down)
        inside = (line >= low) & (line < high) & (col >= right)
        for i, diff in enumerate(half_diffs(side[k].astype(jnp.float32), lasts[k])):
            moved = turned(diff, jnp.where(y == 0, down, half + down), right)
            sums[i] = sums[i] + jnp.where(inside, decay_rate ** (frames - k) * moved, 0.0)
    if rows > part:
        pad = jnp.zeros((rows - part, width), jnp.float32)
        sums = [jnp.concatenate([v, pad], axis=0) for v in sums]
    return sums


def z_kernel(
    sh_ref, phases_ref, side_ref, next_ref, got_ref, g_ref, loc_ref, own_ref, other_ref, wind_ref
):
    frames, block, _ = phases_ref.shape
    rows = own_ref.shape[1]
    y = lax.axis_index("tm") % 2
    shifts = [(sh_ref[2 * k], sh_ref[2 * k + 1]) for k in range(frames)]
    lasts = [next_ref[k : k + 1] for k in range(frames)]
    own = half_products(half_phases(phases_ref, y), lasts, shifts, y, rows)
    at = got_ref.shape[0] - 8
    spot = at + 3 + frames
    shifts = [
        tuple(got_ref[spot, 2 * k + i].astype(jnp.int32) for i in range(2)) for k in range(frames)
    ]
    lasts = [got_ref[at + 3 + k : at + 4 + k] for k in range(frames)]
    other = half_products(side_ref[...], lasts, shifts, y, rows)
    winds = [jnp.float32(0.0), jnp.float32(0.0)]
    for k in range(frames - 1):
        prior = loc_ref[k] - g_ref[k, :block]
        for i, diff in enumerate(
            half_diffs(phases_ref[k].astype(jnp.float32), next_ref[k : k + 1])
        ):
            winds[i] = winds[i] + jnp.sum(prior * diff)
    for i in range(2):
        own_ref[i] = own[i]
        other_ref[i] = other[i]
        wind_ref[i] = winds[i]


def combine_kernel(
    frames, sh_ref, keep_ref, sent_ref, got_ref, near_ref, far_ref,
    late_ref, incl_ref, excl_ref, send_ref, info_ref,
):
    tm = lax.axis_index("tm")
    y = tm % 2
    there = tm // 2 + 1 < lax.axis_size("tm") // 2
    weight = decay_rate**frames
    keep, got = keep_ref[...], unpack(got_ref)
    early = jnp.where(y == 0, keep, got)
    late = jnp.where(y == 0, got, keep)
    late_ref[...] = late
    own = own_shifts(sh_ref, 0, frames)
    other = shift_of(got_ref)
    first = [jnp.where(y == 0, own[i], other[i]) for i in range(2)]
    total = [own[i] + other[i] for i in range(2)]
    near, far = unpack(near_ref), unpack(far_ref)
    near_shift, far_shift = shift_of(near_ref), shift_of(far_ref)
    next_first = [jnp.where(y == 0, near_shift[i], far_shift[i]) for i in range(2)]
    next_late = jnp.where(y == 0, far, near)
    following = jnp.where(y == 0, near, far) + weight * back(next_late, *next_first)
    following = jnp.where(there, following, 0.0)
    excl_ref[...] = following
    both = early + weight * back(late, *first) + weight * weight * back(following, *total)
    incl_ref[...] = both
    for i in range(2):
        info_ref[i] = total[i] - first[i]
        info_ref[2 + i] = total[i]
    power = jnp.maximum(power_of(sent_ref), power_of(got_ref))
    further = jnp.maximum(power_of(near_ref), power_of(far_ref))
    power = jnp.where(there, jnp.maximum(power, further), power)
    span = [total[i] + near_shift[i] + far_shift[i] for i in range(2)]
    pack(send_ref, both, power + 2.0, *span)


def from_pairs(reach, sent_ref, got_ref):
    pair = lax.axis_index("tm") // 2
    there = pair + reach < lax.axis_size("tm") // 2
    power = power_of(sent_ref)
    power = jnp.where(there, jnp.maximum(power, power_of(got_ref)), power)
    return jnp.where(there, unpack(got_ref), 0.0), power


def step_kernel(frames, reach, info_ref, both_ref, excl_in, sent_ref, got_ref, *refs):
    incl_ref, excl_ref, send_ref = refs
    got, power = from_pairs(reach, sent_ref, got_ref)
    span, more = shift_of(sent_ref), shift_of(got_ref)
    both = both_ref[...] + decay_rate ** (2 * frames * reach) * back(got, *span)
    incl_ref[...] = both
    apart = [span[i] - info_ref[2 + i] for i in range(2)]
    excl_ref[...] = excl_in[...] + decay_rate ** (2 * frames * (reach - 1)) * back(got, *apart)
    pack(send_ref, both, power + 1.0, span[0] + more[0], span[1] + more[1])


def carry_kernel(
    frames, reach, info_ref, wind_in, late_ref, excl_ref, sent_ref, got_ref, own_ref, other_ref,
    keep_ref, send_ref, wind_ref,
):
    y = lax.axis_index("tm") % 2
    got, power = from_pairs(reach, sent_ref, got_ref)
    span = shift_of(sent_ref)
    apart = [span[i] - info_ref[2 + i] for i in range(2)]
    late = excl_ref[...] + decay_rate ** (2 * frames * (reach - 1)) * back(got, *apart)
    early = late_ref[...] + decay_rate**frames * back(late, info_ref[0], info_ref[1])
    keep = jnp.where(y == 0, early, late)
    send = jnp.where(y == 0, late, early)
    keep_ref[...] = keep
    pack(send_ref, send, power + 2.0)
    sums = [
        wind_in[i] + jnp.sum(keep * own_ref[i] + send * other_ref[i]) for i in range(2)
    ]
    lane = lax.broadcasted_iota(jnp.int32, wind_ref.shape, 2)
    wind_ref[...] = jnp.where(lane == 0, sums[0], jnp.where(lane == 1, sums[1], 0.0))


def final_kernel(sh_ref, keep_ref, got_ref, loc_ref, adj_ref):
    frames, block, _ = loc_ref.shape
    y = lax.axis_index("tm") % 2
    keep, got = keep_ref[...], unpack(got_ref)
    low = jnp.where(y == 0, keep, got)
    high = jnp.where(y == 0, got, keep)
    field = jnp.concatenate([low[: block // 2], high], axis=0)
    for k in reversed(range(frames)):
        moved = back(field, *own_shifts(sh_ref, k, frames))[:block]
        adj_ref[k] = loc_ref[k] + decay_rate ** (frames - k) * moved


def swap(value, axis, bit):
    count = lax.axis_size(axis)
    return lax.ppermute(value, axis, [(s, s ^ bit) for s in range(count)])


def gather_rows(value):
    count = lax.axis_size("rows")
    held = {0: value}
    bit = count // 2
    while bit:
        for d, v in list(held.items()):
            held[d ^ bit] = swap(v, "rows", bit)
        bit //= 2
    return [held[d] for d in range(count)]


def permute_16(value, target):
    count = lax.axis_size("tm")
    route = [(s, target(s)) for s in range(count) if 0 <= target(s) < count]
    return lax.ppermute(value.astype(jnp.float16), "tm", route).astype(jnp.float32)


def kernel_call(body, vmem_mib, out_shape, in_specs, out_specs, cost=0):
    estimate = pl.CostEstimate(flops=0, bytes_accessed=cost, transcendentals=0) if cost else None
    return pl.pallas_call(
        body,
        out_shape=out_shape,
        in_specs=in_specs,
        out_specs=out_specs,
        cost_estimate=estimate,
        compiler_params=pltpu.CompilerParams(vmem_limit_bytes=vmem_mib << 20),
    )


def on_device(phases, focal_data, shifts, pupil_mask):
    frames, block, width = phases.shape
    n_rows = lax.axis_size("rows")
    n_tm = lax.axis_size("tm")
    frames_all = frames * n_tm
    focal = focal_data.shape[3]
    reach_rows = -(-min(frames_all // 2, width // (4 * n_rows)) // 8) * 8
    halo = -(-reach_rows // 16) * 16
    rows = block + halo
    part = block // 2 + reach_rows
    pairs = n_tm // 2
    half = focal // 2
    cs = tables(width, focal)
    tt = np.concatenate([cs.T, np.zeros((halo, 2 * focal), cs.dtype)], axis=0)
    order = np.concatenate([np.arange(half), half + (half - np.arange(half)) % half])
    cs_turned = np.concatenate([cs[order], cs[focal + order]], axis=0)
    y_table = np.concatenate([cs[:half], cs[focal : focal + half]], axis=0).T
    flip = np.zeros((half, half), cs.dtype)
    flip[(half - np.arange(half)) % half, np.arange(half)] = 1
    own = shifts.reshape(2 * frames)
    vmem = pl.BlockSpec(memory_space=pltpu.VMEM)
    smem = pl.BlockSpec(memory_space=pltpu.SMEM)
    hbm = pl.BlockSpec(memory_space=pltpu.HBM)
    kept = [tt, cs, cs_turned, flip]
    side_shape = (frames, block // 2 + 8, width)
    y, *kept, side = pl.pallas_call(
        functools.partial(y_kernel, halo),
        out_shape=[
            jax.ShapeDtypeStruct((frames * block + 16 + halo * width // focal, focal), jnp.bfloat16)
        ]
        + [jax.ShapeDtypeStruct(t.shape, jnp.bfloat16) for t in kept]
        + [jax.ShapeDtypeStruct(side_shape, jnp.bfloat16)],
        in_specs=[hbm] * (3 + len(kept)),
        out_specs=[vmem] * (2 + len(kept)),
        scratch_shapes=[
            pltpu.VMEM(phases.shape, phases.dtype),
            pltpu.VMEM(pupil_mask.shape, pupil_mask.dtype),
            pltpu.VMEM(y_table.shape, y_table.dtype),
            pltpu.SemaphoreType.DMA((3 + len(kept),)),
        ],
        compiler_params=pltpu.CompilerParams(vmem_limit_bytes=8 << 20),
        name="transform",
    )(*[pltpu.with_memory_space_constraint(t, pltpu.HBM) for t in (phases, pupil_mask, y_table, *kept)])
    d_parts = gather_rows(focal_data)
    m_parts = gather_rows(y)
    side = swap(side, "tm", 1)
    field = jax.ShapeDtypeStruct((frames, block, width), jnp.float32)
    pair = jax.ShapeDtypeStruct((2,), jnp.float32)
    grads, next_rows = pl.pallas_call(
        functools.partial(grad_kernel, n_rows, halo),
        out_shape=(
            jax.ShapeDtypeStruct((frames, rows, width), jnp.float32),
            jax.ShapeDtypeStruct((-(-frames // 8) * 8, width), jnp.float32),
        ),
        in_specs=[vmem] * (2 * n_rows + 5),
        out_specs=(vmem, vmem),
        scratch_shapes=[
            pltpu.VMEM((frames, width, focal), jnp.bfloat16),
            pltpu.VMEM((16, width), jnp.bfloat16),
            pltpu.VMEM((frames, 2, focal, focal), jnp.bfloat16),
            pltpu.VMEM((2 * focal, 2 * focal), jnp.bfloat16),
            pltpu.VMEM((frames, rows, 2 * focal), jnp.bfloat16),
            pltpu.VMEM((halo, width), jnp.float32),
        ],
        compiler_params=pltpu.CompilerParams(vmem_limit_bytes=24 << 20),
        name="grad",
    )(*m_parts, *d_parts, pupil_mask, *kept)
    half_field = jax.ShapeDtypeStruct((part, width), jnp.float32)
    message = jax.ShapeDtypeStruct((part + 8, width), jnp.float32)
    loc, keep, send_keep, send = kernel_call(
        segment_kernel, 12,
        (field, half_field, message, message), [smem, vmem, vmem], (vmem,) * 4,
    )(own, grads, next_rows)
    near = permute_16(send_keep, lambda s: s - 2)
    far = permute_16(send, lambda s: (s - 2) ^ 1)
    got = permute_16(send, lambda s: s ^ 1)
    late, both, excl, send, info = kernel_call(
        functools.partial(combine_kernel, frames), 6,
        (half_field, half_field, half_field, message, jax.ShapeDtypeStruct((4,), jnp.int32)),
        [smem] + [vmem] * 5, (vmem, vmem, vmem, vmem, smem),
    )(own, keep, send, got, near, far)
    products = jax.ShapeDtypeStruct((2, part, width), jnp.float32)
    own_z, other_z, wind_local = kernel_call(
        z_kernel, 12, (products, products, pair), [smem] + [vmem] * 6,
        (vmem, vmem, smem),
    )(own, phases, side, next_rows, got, grads, loc)
    reach = 2
    while 2 * reach < pairs:
        got = permute_16(send, lambda s, r=reach: s - 2 * r)
        both, excl, send = kernel_call(
            functools.partial(step_kernel, frames, reach), 6,
            (half_field, half_field, message), [smem] + [vmem] * 4, (vmem, vmem, vmem),
        )(info, both, excl, send, got)
        reach *= 2
    got = permute_16(send, lambda s: s - 2 * reach)
    n_all = n_tm * n_rows
    keep, send, wind = kernel_call(
        functools.partial(carry_kernel, frames, reach), 8,
        (half_field, message, jax.ShapeDtypeStruct((n_all, 1, LANES), jnp.float32)),
        [smem, smem] + [vmem] * 6, (vmem, vmem, vmem),
    )(info, wind_local, late, excl, send, got, own_z, other_z)
    winds = lax.all_to_all(wind, ("tm", "rows"), 0, 0)
    got = permute_16(send, lambda s: s ^ 1)
    adjoint = kernel_call(
        final_kernel, 8, field, [smem, vmem, vmem, vmem], vmem,
        cost=12 * frames * block * width,
    )(own, keep, got, loc)
    wind_grad = -jnp.sum(winds[:, 0, :2], axis=0) / (width * frames_all)
    return adjoint, wind_grad


def solution(mesh):
    in_specs = (P("tm", "rows", None), P("tm", None, "rows", None), P("tm", None), P("rows", None))
    out_specs = (P("tm", "rows", None), P())

    return jax.shard_map(
        on_device, mesh=mesh, in_specs=in_specs, out_specs=out_specs, check_vma=False
    )
```

```python
import functools
import math

import jax
import jax.numpy as jnp
import numpy as np
from jax import lax
from jax.experimental import pallas as pl
from jax.experimental.pallas import tpu as pltpu
from jax.sharding import PartitionSpec as P

decay_rate = 0.999
LANES = 128


def tables(pupil, focal):
    focal_pos = np.arange(focal) - focal // 2
    pupil_pos = np.arange(pupil) - pupil // 2
    turns = np.mod(focal_pos[:, None] * pupil_pos[None, :], 2 * pupil)
    angle = turns.astype(np.float32) * np.float32(math.pi / pupil)
    factor = np.float32(1.0 / math.sqrt(pupil))
    cos_t = (np.cos(angle) * factor).astype(jnp.bfloat16)
    sin_t = (-np.sin(angle) * factor).astype(jnp.bfloat16)
    return np.concatenate([cos_t, sin_t], axis=0)


def dot(a, b):
    return jnp.dot(a, b, preferred_element_type=jnp.float32)


def turned(value, down, right):
    value = pltpu.roll(value, lax.rem(down, value.shape[0]), 0)
    return pltpu.roll(value, lax.rem(right, value.shape[1]), 1)


def columns(shape):
    return lax.broadcasted_iota(jnp.int32, shape, 1)


def y_kernel(reach_rows, phases_hbm, mask_hbm, half_hbm, *refs):
    count = (len(refs) - 6) // 2
    y_ref, side_ref = refs[count], refs[-5]
    phases_ref, mask_ref, half_ref, sem = refs[-4:]
    ins = [(phases_hbm, phases_ref), (mask_hbm, mask_ref), (half_hbm, half_ref)]
    copies = [(refs[i], refs[count + 1 + i]) for i in range(count)]
    copies = [
        pltpu.make_async_copy(src, dst, sem.at[i]) for i, (src, dst) in enumerate(ins + copies)
    ]
    for copy in copies:
        copy.start()
    for copy in copies[:3]:
        copy.wait()
    frames, block, width = phases_ref.shape
    focal = y_ref.shape[1]
    parts = width // focal
    live = mask_ref[...] == 1
    zero_freq = jnp.full((16, width), zero_freq_value(width), jnp.bfloat16)
    row = lax.broadcasted_iota(jnp.int32, (16, block), 0)
    rows = lax.broadcasted_iota(jnp.int32, (16, focal), 0)
    dc = jnp.zeros((16, block), jnp.float32)
    edge = jnp.zeros((16, focal), jnp.float32)
    for k in range(frames):
        masked = jnp.where(live, phases_ref[k].astype(jnp.float32), 0.0).astype(jnp.bfloat16)
        y_ref[k * block : (k + 1) * block] = dot(masked, half_ref[...]).astype(jnp.bfloat16)
        dc = jnp.where(row == k, dot_t(zero_freq, masked), dc)
        top = phases_ref[k, :8].astype(jnp.float32)[:1]
        for i in range(parts):
            here = jnp.broadcast_to(top[:, i * focal : (i + 1) * focal], edge.shape)
            edge = jnp.where(rows == frames + k * parts + i, here, edge)
    at = frames * block
    y_ref[at : at + 16] = edge.astype(jnp.bfloat16)
    y_ref[at : at + 16, :block] = (edge[:, :block] + dc).astype(jnp.bfloat16)
    at = at + 16
    mask = mask_ref[:reach_rows].astype(jnp.float32).astype(jnp.bfloat16)
    for i in range(parts):
        here = slice(at + i * reach_rows, at + (i + 1) * reach_rows)
        y_ref[here] = mask[:, i * focal : (i + 1) * focal]
    side_ref[...] = half_phases(phases_ref, 1 - lax.axis_index("tm") % 2)
    for copy in copies[3:]:
        copy.wait()


def half_phases(phases_ref, y):
    block = phases_ref.shape[1]
    part = block // 2 + 8
    low = phases_ref[:, :part].astype(jnp.float32)
    high = phases_ref[:, block - part :].astype(jnp.float32)
    return jnp.where(y == 0, low, high).astype(jnp.bfloat16)


def zero_freq_value(width):
    return float(np.float32(np.float32(1.0 / math.sqrt(width)).astype(jnp.bfloat16)))


def dot_t(a, b):
    return lax.dot_general(a, b, (((1,), (1,)), ((), ())), preferred_element_type=jnp.float32)


def grad_kernel(n_rows, reach_rows, halo, *refs):
    m_refs, d_refs = refs[:n_rows], refs[n_rows : 2 * n_rows]
    mask_ref, tt_ref, cs_ref, turned_ref, flip_ref = refs[2 * n_rows : 2 * n_rows + 5]
    g_ref, next_ref = refs[2 * n_rows + 5 : 2 * n_rows + 7]
    y_ref, dc_ref, d_ref, r_ref, w_ref, over_ref = refs[2 * n_rows + 7 :]
    frames = w_ref.shape[0]
    block, width = mask_ref.shape
    focal = cs_ref.shape[0] // 2
    parts = width // focal
    half = focal // 2
    part = focal // n_rows
    rows = block + halo
    me = lax.axis_index("rows")
    over_ref[...] = jnp.zeros_like(over_ref)
    next_ref[...] = jnp.zeros_like(next_ref)
    for d in range(1, n_rows):

        @pl.when((me ^ d) == me + 1)
        def _():
            at = frames * block
            edge = m_refs[d][at : at + 16].astype(jnp.float32)
            for k in range(frames):
                for i in range(parts):
                    line = frames + k * parts + i
                    next_ref[k : k + 1, i * focal : (i + 1) * focal] = edge[line : line + 1]
            at = at + 16
            for i in range(parts):
                over_ref[:reach_rows, i * focal : (i + 1) * focal] = m_refs[d][
                    at + i * reach_rows : at + (i + 1) * reach_rows
                ].astype(jnp.float32)

    for d in range(n_rows):
        at = pl.multiple_of((me ^ d) * block, block)
        at_q = pl.multiple_of((me ^ d) * part, part)
        for k in range(frames):
            y_ref[k, pl.ds(at, block), :] = m_refs[d][k * block : (k + 1) * block]
            d_ref[k, :, pl.ds(at_q, part), :] = d_refs[d][k]
        dc_ref[:, pl.ds(at, block)] = m_refs[d][frames * block : frames * block + 16, :block]
    dc = dot_t(cs_ref[...], dc_ref[...])
    first = columns((focal, half)) == 0
    for k in range(frames):
        pq = dot(cs_ref[...], y_ref[k])
        c_real, c_imag = pq[:focal, :half], pq[:focal, half:]
        s_real, s_imag = pq[focal:, :half], pq[focal:, half:]
        e_real = (c_real - s_imag, jnp.where(first, dc[:focal, k : k + 1], c_real + s_imag))
        e_imag = (c_imag + s_real, jnp.where(first, dc[focal:, k : k + 1], s_real - c_imag))
        for i in range(2):
            at = slice(i * half, (i + 1) * half)
            real, imag = d_ref[k, 0, :, at], d_ref[k, 1, :, at]
            if i:
                real, imag = dot(real, flip_ref[...]), dot(imag, flip_ref[...])
            real = (real.astype(jnp.float32) - e_real[i]).astype(jnp.bfloat16)
            imag = (imag.astype(jnp.float32) - e_imag[i]).astype(jnp.bfloat16)
            r_ref[:focal, i * half : (i + 1) * half] = real
            r_ref[:focal, focal + i * half : focal + (i + 1) * half] = imag
            r_ref[focal:, i * half : (i + 1) * half] = imag
            r_ref[focal:, focal + i * half : focal + (i + 1) * half] = -real
        rows_t = tt_ref[pl.ds(pl.multiple_of(me * block, block), rows), :]
        w_ref[k] = dot(rows_t, r_ref[...]).astype(jnp.bfloat16)
    live = mask_ref[...] == 1
    live_over = over_ref[...] == 1.0
    for k in range(frames):
        g = dot(w_ref[k], turned_ref[...])
        g_ref[k, :block] = jnp.where(live, g[:block], 0.0)
        g_ref[k, block:] = jnp.where(live_over, g[block:], 0.0)


def halves(value, rows, start, y):
    low, high = value[:rows], value[start : start + rows]
    return jnp.where(y == 0, low, high), jnp.where(y == 0, high, low)


def back(value, down, right):
    rows, width = value.shape
    row = lax.broadcasted_iota(jnp.int32, value.shape, 0)
    inside = (columns(value.shape) < width - right) & (row < rows - down)
    return jnp.where(inside, turned(value, rows - down, width - right), 0.0)


def own_shifts(sh_ref, first, stop):
    down, right = jnp.int32(0), jnp.int32(0)
    for k in range(first, stop):
        down, right = down + sh_ref[2 * k], right + sh_ref[2 * k + 1]
    return down, right


def exponent(value, width):
    top = jnp.full((8, width), jnp.maximum(jnp.max(jnp.abs(value)), 1e-30))
    return jnp.ceil(jnp.log2(top))[:1]


def pack(ref, value, power, down=0, right=0, more=()):
    rows = value.shape[0]
    ref[:rows] = value * jnp.exp2(-power)
    line = lax.broadcasted_iota(jnp.int32, (8, value.shape[1]), 0)
    shift = jnp.where(line == 1, down, right).astype(jnp.float32)
    tail = jnp.where(line == 0, power, shift)
    for i, extra in enumerate(more):
        tail = jnp.where(line == 3 + i, extra, tail)
    ref[rows:] = tail


def power_of(ref):
    rows = ref.shape[0] - 8
    return ref[rows : rows + 1]


def shift_of(ref):
    rows = ref.shape[0] - 8
    return ref[rows + 1, 0].astype(jnp.int32), ref[rows + 2, 0].astype(jnp.int32)


def unpack(ref):
    return ref[: ref.shape[0] - 8] * jnp.exp2(power_of(ref))


def segment_kernel(sh_ref, g_ref, next_ref, loc_ref, keep_ref, send_keep_ref, send_ref):
    frames, block, _ = loc_ref.shape
    lam = g_ref[frames - 1]
    loc_ref[frames - 1] = lam[:block]
    for k in reversed(range(frames - 1)):
        lam = g_ref[k] + decay_rate * back(lam, sh_ref[2 * k], sh_ref[2 * k + 1])
        loc_ref[k] = lam[:block]
    keep, send = halves(lam, keep_ref.shape[0], block // 2, lax.axis_index("tm") % 2)
    keep_ref[...] = keep
    power = exponent(lam, lam.shape[1])
    shift = own_shifts(sh_ref, 0, frames)
    pack(send_keep_ref, keep, power, *shift)
    each = jnp.zeros((1, lam.shape[1]), jnp.float32)
    lane = columns(each.shape)
    for i in range(2 * frames):
        each = jnp.where(lane == i, sh_ref[i].astype(jnp.float32), each)
    more = [next_ref[k : k + 1] for k in range(frames)] + [each]
    pack(send_ref, send, power, *shift, more)


def half_diffs(here, last):
    rows, width = here.shape
    row = lax.broadcasted_iota(jnp.int32, here.shape, 0)
    below = jnp.where(row == rows - 1, last, pltpu.roll(here, rows - 1, 0))
    right = jnp.where(columns(here.shape) == width - 1, 0.0, pltpu.roll(here, width - 1, 1))
    return below - here, right - here


def half_products(side, lasts, shifts, y, rows):
    frames, part, width = side.shape
    half = part - 8
    line = lax.broadcasted_iota(jnp.int32, (part, width), 0)
    col = columns((part, width))
    sums = [jnp.zeros((part, width), jnp.float32) for _ in range(2)]
    down, right = jnp.int32(0), jnp.int32(0)
    for k in reversed(range(frames)):
        down, right = down + shifts[k][0], right + shifts[k][1]
        low = jnp.where(y == 0, down, 0)
        high = jnp.where(y == 0, half, half + down)
        inside = (line >= low) & (line < high) & (col >= right)
        for i, diff in enumerate(half_diffs(side[k].astype(jnp.float32), lasts[k])):
            moved = turned(diff, jnp.where(y == 0, down, half + down), right)
            sums[i] = sums[i] + jnp.where(inside, decay_rate ** (frames - k) * moved, 0.0)
    if rows > part:
        pad = jnp.zeros((rows - part, width), jnp.float32)
        sums = [jnp.concatenate([v, pad], axis=0) for v in sums]
    return sums


def z_kernel(
    sh_ref, phases_ref, side_ref, next_ref, got_ref, g_ref, loc_ref, own_ref, other_ref, wind_ref
):
    frames, block, _ = phases_ref.shape
    rows = own_ref.shape[1]
    y = lax.axis_index("tm") % 2
    shifts = [(sh_ref[2 * k], sh_ref[2 * k + 1]) for k in range(frames)]
    lasts = [next_ref[k : k + 1] for k in range(frames)]
    own = half_products(half_phases(phases_ref, y), lasts, shifts, y, rows)
    at = got_ref.shape[0] - 8
    spot = at + 3 + frames
    shifts = [
        tuple(got_ref[spot, 2 * k + i].astype(jnp.int32) for i in range(2)) for k in range(frames)
    ]
    lasts = [got_ref[at + 3 + k : at + 4 + k] for k in range(frames)]
    other = half_products(side_ref[...], lasts, shifts, y, rows)
    winds = [jnp.float32(0.0), jnp.float32(0.0)]
    for k in range(frames - 1):
        prior = loc_ref[k] - g_ref[k, :block]
        for i, diff in enumerate(
            half_diffs(phases_ref[k].astype(jnp.float32), next_ref[k : k + 1])
        ):
            winds[i] = winds[i] + jnp.sum(prior * diff)
    for i in range(2):
        own_ref[i] = own[i]
        other_ref[i] = other[i]
        wind_ref[i] = winds[i]


def combine_kernel(
    frames, sh_ref, keep_ref, sent_ref, got_ref, near_ref, far_ref,
    late_ref, incl_ref, excl_ref, send_ref, info_ref,
):
    tm = lax.axis_index("tm")
    y = tm % 2
    there = tm // 2 + 1 < lax.axis_size("tm") // 2
    weight = decay_rate**frames
    keep, got = keep_ref[...], unpack(got_ref)
    early = jnp.where(y == 0, keep, got)
    late = jnp.where(y == 0, got, keep)
    late_ref[...] = late
    own = own_shifts(sh_ref, 0, frames)
    other = shift_of(got_ref)
    first = [jnp.where(y == 0, own[i], other[i]) for i in range(2)]
    total = [own[i] + other[i] for i in range(2)]
    near, far = unpack(near_ref), unpack(far_ref)
    near_shift, far_shift = shift_of(near_ref), shift_of(far_ref)
    next_first = [jnp.where(y == 0, near_shift[i], far_shift[i]) for i in range(2)]
    next_late = jnp.where(y == 0, far, near)
    following = jnp.where(y == 0, near, far) + weight * back(next_late, *next_first)
    following = jnp.where(there, following, 0.0)
    excl_ref[...] = following
    both = early + weight * back(late, *first) + weight * weight * back(following, *total)
    incl_ref[...] = both
    for i in range(2):
        info_ref[i] = total[i] - first[i]
        info_ref[2 + i] = total[i]
    power = jnp.maximum(power_of(sent_ref), power_of(got_ref))
    further = jnp.maximum(power_of(near_ref), power_of(far_ref))
    power = jnp.where(there, jnp.maximum(power, further), power)
    span = [total[i] + near_shift[i] + far_shift[i] for i in range(2)]
    pack(send_ref, both, power + 2.0, *span)


def from_pairs(reach, sent_ref, got_ref):
    pair = lax.axis_index("tm") // 2
    there = pair + reach < lax.axis_size("tm") // 2
    power = power_of(sent_ref)
    power = jnp.where(there, jnp.maximum(power, power_of(got_ref)), power)
    return jnp.where(there, unpack(got_ref), 0.0), power


def step_kernel(frames, reach, info_ref, both_ref, excl_in, sent_ref, got_ref, *refs):
    incl_ref, excl_ref, send_ref = refs
    got, power = from_pairs(reach, sent_ref, got_ref)
    span, more = shift_of(sent_ref), shift_of(got_ref)
    both = both_ref[...] + decay_rate ** (2 * frames * reach) * back(got, *span)
    incl_ref[...] = both
    apart = [span[i] - info_ref[2 + i] for i in range(2)]
    excl_ref[...] = excl_in[...] + decay_rate ** (2 * frames * (reach - 1)) * back(got, *apart)
    pack(send_ref, both, power + 1.0, span[0] + more[0], span[1] + more[1])


def carry_kernel(
    frames, reach, info_ref, wind_in, late_ref, excl_ref, sent_ref, got_ref, own_ref, other_ref,
    keep_ref, send_ref, wind_ref,
):
    y = lax.axis_index("tm") % 2
    got, power = from_pairs(reach, sent_ref, got_ref)
    span = shift_of(sent_ref)
    apart = [span[i] - info_ref[2 + i] for i in range(2)]
    late = excl_ref[...] + decay_rate ** (2 * frames * (reach - 1)) * back(got, *apart)
    early = late_ref[...] + decay_rate**frames * back(late, info_ref[0], info_ref[1])
    keep = jnp.where(y == 0, early, late)
    send = jnp.where(y == 0, late, early)
    keep_ref[...] = keep
    pack(send_ref, send, power + 2.0)
    sums = [
        wind_in[i] + jnp.sum(keep * own_ref[i] + send * other_ref[i]) for i in range(2)
    ]
    lane = lax.broadcasted_iota(jnp.int32, wind_ref.shape, 2)
    wind_ref[...] = jnp.where(lane == 0, sums[0], jnp.where(lane == 1, sums[1], 0.0))


def final_kernel(sh_ref, keep_ref, got_ref, loc_ref, adj_ref):
    frames, block, _ = loc_ref.shape
    y = lax.axis_index("tm") % 2
    keep, got = keep_ref[...], unpack(got_ref)
    low = jnp.where(y == 0, keep, got)
    high = jnp.where(y == 0, got, keep)
    field = jnp.concatenate([low[: block // 2], high], axis=0)
    for k in reversed(range(frames)):
        moved = back(field, *own_shifts(sh_ref, k, frames))[:block]
        adj_ref[k] = loc_ref[k] + decay_rate ** (frames - k) * moved


def swap(value, axis, bit):
    count = lax.axis_size(axis)
    return lax.ppermute(value, axis, [(s, s ^ bit) for s in range(count)])


def gather_rows(value):
    count = lax.axis_size("rows")
    held = {0: value}
    bit = count // 2
    while bit:
        for d, v in list(held.items()):
            held[d ^ bit] = swap(v, "rows", bit)
        bit //= 2
    return [held[d] for d in range(count)]


def permute_16(value, target):
    count = lax.axis_size("tm")
    route = [(s, target(s)) for s in range(count) if 0 <= target(s) < count]
    return lax.ppermute(value.astype(jnp.float16), "tm", route).astype(jnp.float32)


def kernel_call(body, vmem_mib, out_shape, in_specs, out_specs, cost=0):
    estimate = pl.CostEstimate(flops=0, bytes_accessed=cost, transcendentals=0) if cost else None
    return pl.pallas_call(
        body,
        out_shape=out_shape,
        in_specs=in_specs,
        out_specs=out_specs,
        cost_estimate=estimate,
        compiler_params=pltpu.CompilerParams(vmem_limit_bytes=vmem_mib << 20),
    )


def on_device(phases, focal_data, shifts, pupil_mask):
    frames, block, width = phases.shape
    n_rows = lax.axis_size("rows")
    n_tm = lax.axis_size("tm")
    frames_all = frames * n_tm
    focal = focal_data.shape[3]
    reach_rows = -(-min(frames_all // 2, width // (4 * n_rows)) // 8) * 8
    halo = -(-reach_rows // 16) * 16
    rows = block + halo
    part = block // 2 + reach_rows
    pairs = n_tm // 2
    half = focal // 2
    cs = tables(width, focal)
    tt = np.concatenate([cs.T, np.zeros((halo, 2 * focal), cs.dtype)], axis=0)
    order = np.concatenate([np.arange(half), half + (half - np.arange(half)) % half])
    cs_turned = np.concatenate([cs[order], cs[focal + order]], axis=0)
    y_table = np.concatenate([cs[:half], cs[focal : focal + half]], axis=0).T
    flip = np.zeros((half, half), cs.dtype)
    flip[(half - np.arange(half)) % half, np.arange(half)] = 1
    own = shifts.reshape(2 * frames)
    vmem = pl.BlockSpec(memory_space=pltpu.VMEM)
    smem = pl.BlockSpec(memory_space=pltpu.SMEM)
    hbm = pl.BlockSpec(memory_space=pltpu.HBM)
    kept = [tt, cs, cs_turned, flip]
    side_shape = (frames, block // 2 + 8, width)
    y, *kept, side = pl.pallas_call(
        functools.partial(y_kernel, reach_rows),
        out_shape=[
            jax.ShapeDtypeStruct(
                (frames * block + 16 + reach_rows * width // focal, focal), jnp.bfloat16
            )
        ]
        + [jax.ShapeDtypeStruct(t.shape, jnp.bfloat16) for t in kept]
        + [jax.ShapeDtypeStruct(side_shape, jnp.bfloat16)],
        in_specs=[hbm] * (3 + len(kept)),
        out_specs=[vmem] * (2 + len(kept)),
        scratch_shapes=[
            pltpu.VMEM(phases.shape, phases.dtype),
            pltpu.VMEM(pupil_mask.shape, pupil_mask.dtype),
            pltpu.VMEM(y_table.shape, y_table.dtype),
            pltpu.SemaphoreType.DMA((3 + len(kept),)),
        ],
        compiler_params=pltpu.CompilerParams(vmem_limit_bytes=8 << 20),
        name="transform",
    )(*[pltpu.with_memory_space_constraint(t, pltpu.HBM) for t in (phases, pupil_mask, y_table, *kept)])
    d_parts = gather_rows(focal_data)
    m_parts = gather_rows(y)
    side = swap(side, "tm", 1)
    field = jax.ShapeDtypeStruct((frames, block, width), jnp.float32)
    pair = jax.ShapeDtypeStruct((2,), jnp.float32)
    grads, next_rows = pl.pallas_call(
        functools.partial(grad_kernel, n_rows, reach_rows, halo),
        out_shape=(
            jax.ShapeDtypeStruct((frames, rows, width), jnp.float32),
            jax.ShapeDtypeStruct((-(-frames // 8) * 8, width), jnp.float32),
        ),
        in_specs=[vmem] * (2 * n_rows + 5),
        out_specs=(vmem, vmem),
        scratch_shapes=[
            pltpu.VMEM((frames, width, focal), jnp.bfloat16),
            pltpu.VMEM((16, width), jnp.bfloat16),
            pltpu.VMEM((frames, 2, focal, focal), jnp.bfloat16),
            pltpu.VMEM((2 * focal, 2 * focal), jnp.bfloat16),
            pltpu.VMEM((frames, rows, 2 * focal), jnp.bfloat16),
            pltpu.VMEM((halo, width), jnp.float32),
        ],
        compiler_params=pltpu.CompilerParams(vmem_limit_bytes=24 << 20),
        name="grad",
    )(*m_parts, *d_parts, pupil_mask, *kept)
    half_field = jax.ShapeDtypeStruct((part, width), jnp.float32)
    message = jax.ShapeDtypeStruct((part + 8, width), jnp.float32)
    loc, keep, send_keep, send = kernel_call(
        segment_kernel, 12,
        (field, half_field, message, message), [smem, vmem, vmem], (vmem,) * 4,
    )(own, grads, next_rows)
    near = permute_16(send_keep, lambda s: s - 2)
    far = permute_16(send, lambda s: (s - 2) ^ 1)
    got = permute_16(send, lambda s: s ^ 1)
    late, both, excl, send, info = kernel_call(
        functools.partial(combine_kernel, frames), 6,
        (half_field, half_field, half_field, message, jax.ShapeDtypeStruct((4,), jnp.int32)),
        [smem] + [vmem] * 5, (vmem, vmem, vmem, vmem, smem),
    )(own, keep, send, got, near, far)
    products = jax.ShapeDtypeStruct((2, part, width), jnp.float32)
    own_z, other_z, wind_local = kernel_call(
        z_kernel, 12, (products, products, pair), [smem] + [vmem] * 6,
        (vmem, vmem, smem),
    )(own, phases, side, next_rows, got, grads, loc)
    reach = 2
    while 2 * reach < pairs:
        got = permute_16(send, lambda s, r=reach: s - 2 * r)
        both, excl, send = kernel_call(
            functools.partial(step_kernel, frames, reach), 6,
            (half_field, half_field, message), [smem] + [vmem] * 4, (vmem, vmem, vmem),
        )(info, both, excl, send, got)
        reach *= 2
    got = permute_16(send, lambda s: s - 2 * reach)
    n_all = n_tm * n_rows
    keep, send, wind = kernel_call(
        functools.partial(carry_kernel, frames, reach), 8,
        (half_field, message, jax.ShapeDtypeStruct((n_all, 1, LANES), jnp.float32)),
        [smem, smem] + [vmem] * 6, (vmem, vmem, vmem),
    )(info, wind_local, late, excl, send, got, own_z, other_z)
    winds = lax.all_to_all(wind, ("tm", "rows"), 0, 0)
    got = permute_16(send, lambda s: s ^ 1)
    adjoint = kernel_call(
        final_kernel, 8, field, [smem, vmem, vmem, vmem], vmem,
        cost=12 * frames * block * width,
    )(own, keep, got, loc)
    wind_grad = -jnp.sum(winds[:, 0, :2], axis=0) / (width * frames_all)
    return adjoint, wind_grad


def solution(mesh):
    in_specs = (P("tm", "rows", None), P("tm", None, "rows", None), P("tm", None), P("rows", None))
    out_specs = (P("tm", "rows", None), P())

    return jax.shard_map(
        on_device, mesh=mesh, in_specs=in_specs, out_specs=out_specs, check_vma=False
    )
```

```python
import functools
import math

import jax
import jax.numpy as jnp
import numpy as np
from jax import lax
from jax.experimental import pallas as pl
from jax.experimental.pallas import tpu as pltpu
from jax.sharding import PartitionSpec as P

decay_rate = 0.999
LANES = 128


def tables(pupil, focal):
    focal_pos = np.arange(focal) - focal // 2
    pupil_pos = np.arange(pupil) - pupil // 2
    turns = np.mod(focal_pos[:, None] * pupil_pos[None, :], 2 * pupil)
    angle = turns.astype(np.float32) * np.float32(math.pi / pupil)
    factor = np.float32(1.0 / math.sqrt(pupil))
    cos_t = (np.cos(angle) * factor).astype(jnp.bfloat16)
    sin_t = (-np.sin(angle) * factor).astype(jnp.bfloat16)
    return np.concatenate([cos_t, sin_t], axis=0)


def dot(a, b):
    return jnp.dot(a, b, preferred_element_type=jnp.float32)


def turned(value, down, right):
    value = pltpu.roll(value, lax.rem(down, value.shape[0]), 0)
    return pltpu.roll(value, lax.rem(right, value.shape[1]), 1)


def columns(shape):
    return lax.broadcasted_iota(jnp.int32, shape, 1)


def y_kernel(reach_rows, phases_hbm, mask_hbm, half_hbm, *refs):
    count = (len(refs) - 6) // 2
    y_ref, side_ref = refs[count], refs[-5]
    phases_ref, mask_ref, half_ref, sem = refs[-4:]
    ins = [(phases_hbm, phases_ref), (mask_hbm, mask_ref), (half_hbm, half_ref)]
    copies = [(refs[i], refs[count + 1 + i]) for i in range(count)]
    copies = [
        pltpu.make_async_copy(src, dst, sem.at[i]) for i, (src, dst) in enumerate(ins + copies)
    ]
    for copy in copies:
        copy.start()
    for copy in copies[:3]:
        copy.wait()
    frames, block, width = phases_ref.shape
    focal = y_ref.shape[1]
    parts = width // focal
    live = mask_ref[...] == 1
    zero_freq = jnp.full((16, width), zero_freq_value(width), jnp.bfloat16)
    row = lax.broadcasted_iota(jnp.int32, (16, block), 0)
    rows = lax.broadcasted_iota(jnp.int32, (16, focal), 0)
    dc = jnp.zeros((16, block), jnp.float32)
    edge = jnp.zeros((16, focal), jnp.float32)
    for k in range(frames):
        masked = jnp.where(live, phases_ref[k].astype(jnp.float32), 0.0).astype(jnp.bfloat16)
        y_ref[k * block : (k + 1) * block] = dot(masked, half_ref[...]).astype(jnp.bfloat16)
        dc = jnp.where(row == k, dot_t(zero_freq, masked), dc)
        top = phases_ref[k, :8].astype(jnp.float32)[:1]
        for i in range(parts):
            here = jnp.broadcast_to(top[:, i * focal : (i + 1) * focal], edge.shape)
            edge = jnp.where(rows == frames + k * parts + i, here, edge)
    at = frames * block
    y_ref[at : at + 16] = edge.astype(jnp.bfloat16)
    y_ref[at : at + 16, :block] = (edge[:, :block] + dc).astype(jnp.bfloat16)
    at = at + 16
    mask = mask_ref[:reach_rows].astype(jnp.float32).astype(jnp.bfloat16)
    for i in range(parts):
        here = slice(at + i * reach_rows, at + (i + 1) * reach_rows)
        y_ref[here] = mask[:, i * focal : (i + 1) * focal]
    side_ref[...] = half_phases(phases_ref, 1 - lax.axis_index("tm") % 2)
    for copy in copies[3:]:
        copy.wait()


def half_phases(phases_ref, y):
    block = phases_ref.shape[1]
    part = block // 2 + 8
    low = phases_ref[:, :part].astype(jnp.float32)
    high = phases_ref[:, block - part :].astype(jnp.float32)
    return jnp.where(y == 0, low, high).astype(jnp.bfloat16)


def zero_freq_value(width):
    return float(np.float32(np.float32(1.0 / math.sqrt(width)).astype(jnp.bfloat16)))


def dot_t(a, b):
    return lax.dot_general(a, b, (((1,), (1,)), ((), ())), preferred_element_type=jnp.float32)


def grad_kernel(n_rows, reach_rows, halo, *refs):
    m_refs, d_refs = refs[:n_rows], refs[n_rows : 2 * n_rows]
    mask_ref, tt_ref, cs_ref, turned_ref, flip_ref = refs[2 * n_rows : 2 * n_rows + 5]
    g_ref, next_ref = refs[2 * n_rows + 5 : 2 * n_rows + 7]
    y_ref, dc_ref, d_ref, r_ref, w_ref, over_ref = refs[2 * n_rows + 7 :]
    frames = w_ref.shape[0]
    block, width = mask_ref.shape
    focal = cs_ref.shape[0] // 2
    parts = width // focal
    half = focal // 2
    part = focal // n_rows
    rows = block + halo
    me = lax.axis_index("rows")
    over_ref[...] = jnp.zeros_like(over_ref)
    next_ref[...] = jnp.zeros_like(next_ref)
    for d in range(1, n_rows):

        @pl.when((me ^ d) == me + 1)
        def _():
            at = frames * block
            edge = m_refs[d][at : at + 16].astype(jnp.float32)
            for k in range(frames):
                for i in range(parts):
                    line = frames + k * parts + i
                    next_ref[k : k + 1, i * focal : (i + 1) * focal] = edge[line : line + 1]
            at = at + 16
            for i in range(parts):
                over_ref[:reach_rows, i * focal : (i + 1) * focal] = m_refs[d][
                    at + i * reach_rows : at + (i + 1) * reach_rows
                ].astype(jnp.float32)

    for d in range(n_rows):
        at = pl.multiple_of((me ^ d) * block, block)
        at_q = pl.multiple_of((me ^ d) * part, part)
        for k in range(frames):
            y_ref[k, pl.ds(at, block), :] = m_refs[d][k * block : (k + 1) * block]
            d_ref[k, :, pl.ds(at_q, part), :] = d_refs[d][k]
        dc_ref[:, pl.ds(at, block)] = m_refs[d][frames * block : frames * block + 16, :block]
    dc = dot_t(cs_ref[...], dc_ref[...])
    first = columns((focal, half)) == 0
    for k in range(frames):
        pq = dot(cs_ref[...], y_ref[k])
        c_real, c_imag = pq[:focal, :half], pq[:focal, half:]
        s_real, s_imag = pq[focal:, :half], pq[focal:, half:]
        e_real = (c_real - s_imag, jnp.where(first, dc[:focal, k : k + 1], c_real + s_imag))
        e_imag = (c_imag + s_real, jnp.where(first, dc[focal:, k : k + 1], s_real - c_imag))
        for i in range(2):
            at = slice(i * half, (i + 1) * half)
            real, imag = d_ref[k, 0, :, at], d_ref[k, 1, :, at]
            if i:
                real, imag = dot(real, flip_ref[...]), dot(imag, flip_ref[...])
            real = (real.astype(jnp.float32) - e_real[i]).astype(jnp.bfloat16)
            imag = (imag.astype(jnp.float32) - e_imag[i]).astype(jnp.bfloat16)
            r_ref[:focal, i * half : (i + 1) * half] = real
            r_ref[:focal, focal + i * half : focal + (i + 1) * half] = imag
            r_ref[focal:, i * half : (i + 1) * half] = imag
            r_ref[focal:, focal + i * half : focal + (i + 1) * half] = -real
        rows_t = tt_ref[pl.ds(pl.multiple_of(me * block, block), rows), :]
        w_ref[k] = dot(rows_t, r_ref[...]).astype(jnp.bfloat16)
    live = mask_ref[...] == 1
    live_over = over_ref[...] == 1.0
    for k in range(frames):
        g = dot(w_ref[k], turned_ref[...])
        g_ref[k, :block] = jnp.where(live, g[:block], 0.0)
        g_ref[k, block:] = jnp.where(live_over, g[block:], 0.0)


def halves(value, rows, start, y):
    low, high = value[:rows], value[start : start + rows]
    return jnp.where(y == 0, low, high), jnp.where(y == 0, high, low)


def back(value, down, right):
    rows, width = value.shape
    row = lax.broadcasted_iota(jnp.int32, value.shape, 0)
    inside = (columns(value.shape) < width - right) & (row < rows - down)
    return jnp.where(inside, turned(value, rows - down, width - right), 0.0)


def own_shifts(sh_ref, first, stop):
    down, right = jnp.int32(0), jnp.int32(0)
    for k in range(first, stop):
        down, right = down + sh_ref[2 * k], right + sh_ref[2 * k + 1]
    return down, right


def exponent(value, width):
    top = jnp.full((8, width), jnp.maximum(jnp.max(jnp.abs(value)), 1e-30))
    return jnp.ceil(jnp.log2(top))[:1]


def pack(ref, value, power, down=0, right=0, more=()):
    rows = value.shape[0]
    ref[:rows] = value * jnp.exp2(-power)
    line = lax.broadcasted_iota(jnp.int32, (8, value.shape[1]), 0)
    shift = jnp.where(line == 1, down, right).astype(jnp.float32)
    tail = jnp.where(line == 0, power, shift)
    for i, extra in enumerate(more):
        tail = jnp.where(line == 3 + i, extra, tail)
    ref[rows:] = tail


def power_of(ref):
    rows = ref.shape[0] - 8
    return ref[rows : rows + 1]


def shift_of(ref):
    rows = ref.shape[0] - 8
    return ref[rows + 1, 0].astype(jnp.int32), ref[rows + 2, 0].astype(jnp.int32)


def unpack(ref):
    return ref[: ref.shape[0] - 8] * jnp.exp2(power_of(ref))


def segment_kernel(sh_ref, g_ref, next_ref, loc_ref, keep_ref, send_keep_ref, send_ref):
    frames, block, _ = loc_ref.shape
    lam = g_ref[frames - 1]
    loc_ref[frames - 1] = lam[:block]
    for k in reversed(range(frames - 1)):
        lam = g_ref[k] + decay_rate * back(lam, sh_ref[2 * k], sh_ref[2 * k + 1])
        loc_ref[k] = lam[:block]
    keep, send = halves(lam, keep_ref.shape[0], block // 2, lax.axis_index("tm") % 2)
    keep_ref[...] = keep
    power = exponent(lam, lam.shape[1])
    shift = own_shifts(sh_ref, 0, frames)
    pack(send_keep_ref, keep, power, *shift)
    each = jnp.zeros((1, lam.shape[1]), jnp.float32)
    lane = columns(each.shape)
    for i in range(2 * frames):
        each = jnp.where(lane == i, sh_ref[i].astype(jnp.float32), each)
    more = [next_ref[k : k + 1] for k in range(frames)] + [each]
    pack(send_ref, send, power, *shift, more)


def half_diffs(here, last):
    rows, width = here.shape
    row = lax.broadcasted_iota(jnp.int32, here.shape, 0)
    below = jnp.where(row == rows - 1, last, pltpu.roll(here, rows - 1, 0))
    right = jnp.where(columns(here.shape) == width - 1, 0.0, pltpu.roll(here, width - 1, 1))
    return below - here, right - here


def half_products(side, lasts, shifts, y, rows):
    frames, part, width = side.shape
    half = part - 8
    line = lax.broadcasted_iota(jnp.int32, (part, width), 0)
    col = columns((part, width))
    sums = [jnp.zeros((part, width), jnp.float32) for _ in range(2)]
    down, right = jnp.int32(0), jnp.int32(0)
    for k in reversed(range(frames)):
        down, right = down + shifts[k][0], right + shifts[k][1]
        low = jnp.where(y == 0, down, 0)
        high = jnp.where(y == 0, half, half + down)
        inside = (line >= low) & (line < high) & (col >= right)
        for i, diff in enumerate(half_diffs(side[k].astype(jnp.float32), lasts[k])):
            moved = turned(diff, jnp.where(y == 0, down, half + down), right)
            sums[i] = sums[i] + jnp.where(inside, decay_rate ** (frames - k) * moved, 0.0)
    if rows > part:
        pad = jnp.zeros((rows - part, width), jnp.float32)
        sums = [jnp.concatenate([v, pad], axis=0) for v in sums]
    return sums


def z_kernel(
    sh_ref, phases_ref, side_ref, next_ref, got_ref, g_ref, loc_ref, own_ref, other_ref, wind_ref
):
    frames, block, _ = phases_ref.shape
    rows = own_ref.shape[1]
    y = lax.axis_index("tm") % 2
    shifts = [(sh_ref[2 * k], sh_ref[2 * k + 1]) for k in range(frames)]
    lasts = [next_ref[k : k + 1] for k in range(frames)]
    own = half_products(half_phases(phases_ref, y), lasts, shifts, y, rows)
    at = got_ref.shape[0] - 8
    spot = at + 3 + frames
    shifts = [
        tuple(got_ref[spot, 2 * k + i].astype(jnp.int32) for i in range(2)) for k in range(frames)
    ]
    lasts = [got_ref[at + 3 + k : at + 4 + k] for k in range(frames)]
    other = half_products(side_ref[...], lasts, shifts, y, rows)
    winds = [jnp.float32(0.0), jnp.float32(0.0)]
    for k in range(frames - 1):
        prior = loc_ref[k] - g_ref[k, :block]
        for i, diff in enumerate(
            half_diffs(phases_ref[k].astype(jnp.float32), next_ref[k : k + 1])
        ):
            winds[i] = winds[i] + jnp.sum(prior * diff)
    for i in range(2):
        own_ref[i] = own[i]
        other_ref[i] = other[i]
        wind_ref[i] = winds[i]


def combine_kernel(
    frames, sh_ref, keep_ref, sent_ref, got_ref, near_ref, far_ref,
    late_ref, excl_ref, send_ref, info_ref, *incl_refs,
):
    tm = lax.axis_index("tm")
    y = tm % 2
    there = tm // 2 + 1 < lax.axis_size("tm") // 2
    weight = decay_rate**frames
    keep, got = keep_ref[...], unpack(got_ref)
    early = jnp.where(y == 0, keep, got)
    late = jnp.where(y == 0, got, keep)
    late_ref[...] = late
    own = own_shifts(sh_ref, 0, frames)
    other = shift_of(got_ref)
    first = [jnp.where(y == 0, own[i], other[i]) for i in range(2)]
    total = [own[i] + other[i] for i in range(2)]
    near, far = unpack(near_ref), unpack(far_ref)
    near_shift, far_shift = shift_of(near_ref), shift_of(far_ref)
    next_first = [jnp.where(y == 0, near_shift[i], far_shift[i]) for i in range(2)]
    next_late = jnp.where(y == 0, far, near)
    following = jnp.where(y == 0, near, far) + weight * back(next_late, *next_first)
    following = jnp.where(there, following, 0.0)
    excl_ref[...] = following
    both = early + weight * back(late, *first) + weight * weight * back(following, *total)
    for ref in incl_refs:
        ref[...] = both
    for i in range(2):
        info_ref[i] = total[i] - first[i]
        info_ref[2 + i] = total[i]
    power = jnp.maximum(power_of(sent_ref), power_of(got_ref))
    further = jnp.maximum(power_of(near_ref), power_of(far_ref))
    power = jnp.where(there, jnp.maximum(power, further), power)
    span = [total[i] + near_shift[i] + far_shift[i] for i in range(2)]
    for i in range(2):
        info_ref[4 + i] = near_shift[i] + far_shift[i]
    pack(send_ref, both, power + 2.0, *span)


def from_pairs(reach, sent_ref, got_ref):
    pair = lax.axis_index("tm") // 2
    there = pair + reach < lax.axis_size("tm") // 2
    power = power_of(sent_ref)
    power = jnp.where(there, jnp.maximum(power, power_of(got_ref)), power)
    return jnp.where(there, unpack(got_ref), 0.0), power


def step_kernel(frames, reach, info_ref, both_ref, excl_in, sent_ref, got_ref, *refs):
    incl_ref, excl_ref, send_ref = refs
    got, power = from_pairs(reach, sent_ref, got_ref)
    span, more = shift_of(sent_ref), shift_of(got_ref)
    both = both_ref[...] + decay_rate ** (2 * frames * reach) * back(got, *span)
    incl_ref[...] = both
    apart = [span[i] - info_ref[2 + i] for i in range(2)]
    excl_ref[...] = excl_in[...] + decay_rate ** (2 * frames * (reach - 1)) * back(got, *apart)
    pack(send_ref, both, power + 1.0, span[0] + more[0], span[1] + more[1])


def carry_kernel(
    frames, reach, info_ref, wind_in, late_ref, excl_ref, sent_ref, got_ref, own_ref, other_ref,
    keep_ref, send_ref, wind_ref,
):
    y = lax.axis_index("tm") % 2
    got, power = from_pairs(reach, sent_ref, got_ref)
    if reach == 2:
        apart = [info_ref[4 + i] for i in range(2)]
    else:
        span = shift_of(sent_ref)
        apart = [span[i] - info_ref[2 + i] for i in range(2)]
    late = excl_ref[...] + decay_rate ** (2 * frames * (reach - 1)) * back(got, *apart)
    early = late_ref[...] + decay_rate**frames * back(late, info_ref[0], info_ref[1])
    keep = jnp.where(y == 0, early, late)
    send = jnp.where(y == 0, late, early)
    keep_ref[...] = keep
    pack(send_ref, send, power + 2.0)
    sums = [
        wind_in[i] + jnp.sum(keep * own_ref[i] + send * other_ref[i]) for i in range(2)
    ]
    lane = lax.broadcasted_iota(jnp.int32, wind_ref.shape, 2)
    wind_ref[...] = jnp.where(lane == 0, sums[0], jnp.where(lane == 1, sums[1], 0.0))


def final_kernel(sh_ref, keep_ref, got_ref, loc_ref, adj_ref):
    frames, block, _ = loc_ref.shape
    y = lax.axis_index("tm") % 2
    keep, got = keep_ref[...], unpack(got_ref)
    low = jnp.where(y == 0, keep, got)
    high = jnp.where(y == 0, got, keep)
    field = jnp.concatenate([low[: block // 2], high], axis=0)
    for k in reversed(range(frames)):
        moved = back(field, *own_shifts(sh_ref, k, frames))[:block]
        adj_ref[k] = loc_ref[k] + decay_rate ** (frames - k) * moved


def swap(value, axis, bit):
    count = lax.axis_size(axis)
    return lax.ppermute(value, axis, [(s, s ^ bit) for s in range(count)])


def gather_rows(value):
    count = lax.axis_size("rows")
    held = {0: value}
    bit = count // 2
    while bit:
        for d, v in list(held.items()):
            held[d ^ bit] = swap(v, "rows", bit)
        bit //= 2
    return [held[d] for d in range(count)]


def permute_16(value, target):
    count = lax.axis_size("tm")
    route = [(s, target(s)) for s in range(count) if 0 <= target(s) < count]
    return lax.ppermute(value.astype(jnp.float16), "tm", route).astype(jnp.float32)


def kernel_call(body, vmem_mib, out_shape, in_specs, out_specs, cost=0):
    estimate = pl.CostEstimate(flops=0, bytes_accessed=cost, transcendentals=0) if cost else None
    return pl.pallas_call(
        body,
        out_shape=out_shape,
        in_specs=in_specs,
        out_specs=out_specs,
        cost_estimate=estimate,
        compiler_params=pltpu.CompilerParams(vmem_limit_bytes=vmem_mib << 20),
    )


def on_device(phases, focal_data, shifts, pupil_mask):
    frames, block, width = phases.shape
    n_rows = lax.axis_size("rows")
    n_tm = lax.axis_size("tm")
    frames_all = frames * n_tm
    focal = focal_data.shape[3]
    reach_rows = -(-min(frames_all // 2, width // (4 * n_rows)) // 8) * 8
    halo = -(-reach_rows // 16) * 16
    rows = block + halo
    part = block // 2 + reach_rows
    pairs = n_tm // 2
    half = focal // 2
    cs = tables(width, focal)
    tt = np.concatenate([cs.T, np.zeros((halo, 2 * focal), cs.dtype)], axis=0)
    order = np.concatenate([np.arange(half), half + (half - np.arange(half)) % half])
    cs_turned = np.concatenate([cs[order], cs[focal + order]], axis=0)
    y_table = np.concatenate([cs[:half], cs[focal : focal + half]], axis=0).T
    flip = np.zeros((half, half), cs.dtype)
    flip[(half - np.arange(half)) % half, np.arange(half)] = 1
    own = shifts.reshape(2 * frames)
    vmem = pl.BlockSpec(memory_space=pltpu.VMEM)
    smem = pl.BlockSpec(memory_space=pltpu.SMEM)
    hbm = pl.BlockSpec(memory_space=pltpu.HBM)
    kept = [tt, cs, cs_turned, flip]
    side_shape = (frames, block // 2 + 8, width)
    y, *kept, side = pl.pallas_call(
        functools.partial(y_kernel, reach_rows),
        out_shape=[
            jax.ShapeDtypeStruct(
                (frames * block + 16 + reach_rows * width // focal, focal), jnp.bfloat16
            )
        ]
        + [jax.ShapeDtypeStruct(t.shape, jnp.bfloat16) for t in kept]
        + [jax.ShapeDtypeStruct(side_shape, jnp.bfloat16)],
        in_specs=[hbm] * (3 + len(kept)),
        out_specs=[vmem] * (2 + len(kept)),
        scratch_shapes=[
            pltpu.VMEM(phases.shape, phases.dtype),
            pltpu.VMEM(pupil_mask.shape, pupil_mask.dtype),
            pltpu.VMEM(y_table.shape, y_table.dtype),
            pltpu.SemaphoreType.DMA((3 + len(kept),)),
        ],
        compiler_params=pltpu.CompilerParams(vmem_limit_bytes=8 << 20),
        name="transform",
    )(*[pltpu.with_memory_space_constraint(t, pltpu.HBM) for t in (phases, pupil_mask, y_table, *kept)])
    d_parts = gather_rows(focal_data)
    m_parts = gather_rows(y)
    side = swap(side, "tm", 1)
    field = jax.ShapeDtypeStruct((frames, block, width), jnp.float32)
    pair = jax.ShapeDtypeStruct((2,), jnp.float32)
    grads, next_rows = pl.pallas_call(
        functools.partial(grad_kernel, n_rows, reach_rows, halo),
        out_shape=(
            jax.ShapeDtypeStruct((frames, rows, width), jnp.float32),
            jax.ShapeDtypeStruct((-(-frames // 8) * 8, width), jnp.float32),
        ),
        in_specs=[vmem] * (2 * n_rows + 5),
        out_specs=(vmem, vmem),
        scratch_shapes=[
            pltpu.VMEM((frames, width, focal), jnp.bfloat16),
            pltpu.VMEM((16, width), jnp.bfloat16),
            pltpu.VMEM((frames, 2, focal, focal), jnp.bfloat16),
            pltpu.VMEM((2 * focal, 2 * focal), jnp.bfloat16),
            pltpu.VMEM((frames, rows, 2 * focal), jnp.bfloat16),
            pltpu.VMEM((halo, width), jnp.float32),
        ],
        compiler_params=pltpu.CompilerParams(vmem_limit_bytes=24 << 20),
        name="grad",
    )(*m_parts, *d_parts, pupil_mask, *kept)
    half_field = jax.ShapeDtypeStruct((part, width), jnp.float32)
    message = jax.ShapeDtypeStruct((part + 8, width), jnp.float32)
    loc, keep, send_keep, send = kernel_call(
        segment_kernel, 12,
        (field, half_field, message, message), [smem, vmem, vmem], (vmem,) * 4,
    )(own, grads, next_rows)
    near = permute_16(send_keep, lambda s: s - 2)
    far = permute_16(send, lambda s: (s - 2) ^ 1)
    got = permute_16(send, lambda s: s ^ 1)
    more = int(pairs > 4)
    late, excl, send, info, *both = kernel_call(
        functools.partial(combine_kernel, frames), 6,
        [half_field, half_field, message, jax.ShapeDtypeStruct((6,), jnp.int32)]
        + [half_field] * more,
        [smem] + [vmem] * 5, [vmem, vmem, vmem, smem] + [vmem] * more,
    )(own, keep, send, got, near, far)
    products = jax.ShapeDtypeStruct((2, part, width), jnp.float32)
    own_z, other_z, wind_local = kernel_call(
        z_kernel, 12, (products, products, pair), [smem] + [vmem] * 6,
        (vmem, vmem, smem),
    )(own, phases, side, next_rows, got, grads, loc)
    reach = 2
    while 2 * reach < pairs:
        got = permute_16(send, lambda s, r=reach: s - 2 * r)
        *both, excl, send = kernel_call(
            functools.partial(step_kernel, frames, reach), 6,
            (half_field, half_field, message), [smem] + [vmem] * 4, (vmem, vmem, vmem),
        )(info, *both, excl, send, got)
        reach *= 2
    got = permute_16(send, lambda s: s - 2 * reach)
    n_all = n_tm * n_rows
    keep, send, wind = kernel_call(
        functools.partial(carry_kernel, frames, reach), 8,
        (half_field, message, jax.ShapeDtypeStruct((n_all, 1, LANES), jnp.float32)),
        [smem, smem] + [vmem] * 6, (vmem, vmem, vmem),
    )(info, wind_local, late, excl, send, got, own_z, other_z)
    winds = lax.all_to_all(wind, ("tm", "rows"), 0, 0)
    got = permute_16(send, lambda s: s ^ 1)
    adjoint = kernel_call(
        final_kernel, 8, field, [smem, vmem, vmem, vmem], vmem,
        cost=12 * frames * block * width,
    )(own, keep, got, loc)
    wind_grad = -jnp.sum(winds[:, 0, :2], axis=0) / (width * frames_all)
    return adjoint, wind_grad


def solution(mesh):
    in_specs = (P("tm", "rows", None), P("tm", None, "rows", None), P("tm", None), P("rows", None))
    out_specs = (P("tm", "rows", None), P())

    return jax.shard_map(
        on_device, mesh=mesh, in_specs=in_specs, out_specs=out_specs, check_vma=False
    )
```
